32 devices in a mesh: row: 4 (over y, core), col: 8 (over z, x).
Axes of the slice: x: 2, y: 2, z: 4, core: 2. Of those that a mesh axis runs over, the one named last changes fastest.
Arguments:
- layer_input: bfloat16 [256, 8192], P('row', 'col'), may hold values from -36 to 36, as said below
- norm_gain: float32 [8192], P('col'), may hold values from 0.1 to 1.9
- w_gate: bfloat16 [8192, 14336], P('col', 'row'), may hold values from -0.09375 to 0.09375
- w_up: bfloat16 [8192, 14336], P('col', 'row'), may hold values from -0.09375 to 0.09375
- w_down: bfloat16 [14336, 8192], P('row', 'col'), may hold values from -0.09375 to 0.09375
- mask_gate: int32 [64, 112], P('col', 'row'), may hold values 0 or 1
- mask_up: int32 [64, 112], P('col', 'row'), may hold values 0 or 1
- mask_down: int32 [112, 64], P('row', 'col'), may hold values 0 or 1
- out_grad: bfloat16 [256, 8192], P('row', 'col'), may hold values from -6 to 6
Outputs:
- layer_out: bfloat16 [256, 8192], P('row', 'col')
- input_grad: bfloat16 [256, 8192], P('row', 'col')
- gain_grad: float32 [8192], P('col')
- gate_wgrad: bfloat16 [8192, 14336], P('col', 'row')
- up_wgrad: bfloat16 [8192, 14336], P('col', 'row')
- down_wgrad: bfloat16 [14336, 8192], P('row', 'col')
The draws below stay inside these ranges and needn't reach their ends.
Inputs may be any that keep to these rules, and one draw needn't show every extreme that they name: `layer_input`: the layer input's rows and features have scales that differ by up to a factor of ten.
All inputs are finite; a program needn't handle non-finite values. No bound on the sum of `mask_gate` or of `mask_up` or of `mask_down` on one device may be relied on, other than what follows from the above.
Results may differ from the reference program's by a relative error of at most 0.02.
Values may be sent and summed in bfloat16 or wider, within the bound.
A program may use at most 192 MiB of HBM per device.

```python
import math
import jax
import jax.numpy as jnp
from jax import lax

D = 8192
FF = 14336
BLK = 128
TOKENS = 256


def draw_layer_input(key, part):
    row_key = jax.random.fold_in(key, 11)
    col_key = jax.random.fold_in(key, 12)
    base_key = jax.random.fold_in(key, 13)
    row_scale = jnp.exp(jax.random.uniform(row_key, (TOKENS, 1), jnp.float32, math.log(0.3), math.log(3.0)))
    col_scale = jnp.exp(jax.random.uniform(col_key, (1, D), jnp.float32, math.log(0.3), math.log(3.0)))
    base = jax.random.truncated_normal(base_key, -4.0, 4.0, (TOKENS, D), jnp.float32)
    return (base * row_scale * col_scale).astype(jnp.bfloat16)


def place_ends(array, key, smallest, largest):
    longest = array.shape.index(max(array.shape))
    spots = []
    for shift in (0, 1):
        where = [jax.random.randint(jax.random.fold_in(key, axis), (), 0, length) for axis, length in enumerate(array.shape)]
        where[longest] = (where[longest] + shift) % array.shape[longest]
        spots.append(tuple(where))
    return array.at[spots[0]].set(smallest).at[spots[1]].set(largest)


def shard_levels(stream_key, shape, split, least, largest):
    def one(dim, blocks):
        draws = jax.random.uniform(jax.random.fold_in(jax.random.fold_in(stream_key, 6), dim), (blocks,), jnp.float32, least / len(split), largest / len(split))
        return jnp.repeat(jnp.exp(draws), shape[dim] // blocks).reshape((-1,) + (1,) * (len(shape) - dim - 1))

    gain = one(*split[0])
    for cut in split[1:]:
        gain = gain * one(*cut)
    return gain


def gaussian(rng, extent, scale, limit, pieces=(), held_as=jnp.bfloat16):
    factor_of = shard_levels(rng, extent, pieces, -0.22, 0.18) if pieces else 1.0
    drawn = jax.random.normal(rng, extent, jnp.float32) * scale * factor_of
    return jnp.minimum(jnp.maximum(drawn, -limit), limit).astype(held_as)


def setup_inputs(seed: int = 0) -> dict:
    splits = jax.random.split(jax.random.key(seed), 10)
    layer_input = draw_layer_input(jax.random.fold_in(splits[9], 71), 0)
    norm_gain = jnp.clip(1.0 + 0.18 * jax.random.normal(splits[1], (D,), jnp.float32), 0.1, 1.9)
    w_gate = gaussian(splits[2], (D, FF), (D // 2) ** -0.5, 0.09375, ((0, 8), (1, 4)))
    w_up = gaussian(splits[3], (D, FF), (D // 2) ** -0.5, 0.09375, ((0, 8), (1, 4)))
    w_down = gaussian(splits[4], (FF, D), (FF // 4) ** -0.5, 0.09375, ((0, 4), (1, 8)))
    mask_gate = place_ends((jax.random.randint(splits[5], (D // BLK, FF // BLK), 0, 2) < 1).astype(jnp.int32), jax.random.fold_in(splits[5], 1), 0, 1)
    mask_up = place_ends((jax.random.randint(splits[6], (D // BLK, FF // BLK), 0, 2) < 1).astype(jnp.int32), jax.random.fold_in(splits[6], 1), 0, 1)
    mask_down = place_ends((jax.random.randint(splits[7], (FF // BLK, D // BLK), 0, 2) < 1).astype(jnp.int32), jax.random.fold_in(splits[7], 1), 0, 1)
    out_grad = gaussian(splits[8], (TOKENS, D), 1.0, 6.0, ((0, 4), (1, 8)))
    return dict(layer_input=layer_input, norm_gain=norm_gain, w_gate=w_gate, w_up=w_up, w_down=w_down, mask_gate=mask_gate, mask_up=mask_up, mask_down=mask_down, out_grad=out_grad)


norm_eps = 1e-05

def apply_mask(weight, mask):
    block_rows, block_cols = mask.shape
    row_count, col_count = weight.shape
    blocks = weight.reshape(block_rows, row_count // block_rows, block_cols, col_count // block_cols)
    keep = mask.astype(weight.dtype)[:, None, :, None]
    return (blocks * keep).reshape(row_count, col_count)

def contract_rows(left, right):
    return lax.dot_general(left, right, (((0,), (0,)), ((), ())), preferred_element_type=jnp.float32)

def contract_cols(left, right):
    return lax.dot_general(left, right, (((1,), (1,)), ((), ())), preferred_element_type=jnp.float32)

def reference(layer_input, norm_gain, w_gate, w_up, w_down, mask_gate, mask_up, mask_down, out_grad):
    x_float = layer_input.astype(jnp.float32)
    scale = lax.rsqrt(lax.optimization_barrier(jnp.sum(x_float * x_float, axis=1)) / D + norm_eps)[:, None]
    normed = (x_float * scale * norm_gain[None, :]).astype(jnp.bfloat16)
    eff_gate = apply_mask(w_gate, mask_gate)
    eff_up = apply_mask(w_up, mask_up)
    eff_down = apply_mask(w_down, mask_down)
    gate = jnp.dot(normed, eff_gate, preferred_element_type=jnp.float32)
    up = jnp.dot(normed, eff_up, preferred_element_type=jnp.float32)
    act = (jax.nn.silu(gate) * up).astype(jnp.bfloat16)
    layer_out = (x_float + jnp.dot(act, eff_down, preferred_element_type=jnp.float32)).astype(jnp.bfloat16)
    act_grad = contract_cols(out_grad, eff_down)
    down_wgrad = apply_mask(contract_rows(act, out_grad), mask_down).astype(jnp.bfloat16)
    sig = jax.nn.sigmoid(gate)
    gate_grad = (act_grad * up * sig * (1.0 + gate * (1.0 - sig))).astype(jnp.bfloat16)
    up_grad = (act_grad * gate * sig).astype(jnp.bfloat16)
    gate_wgrad = apply_mask(contract_rows(normed, gate_grad), mask_gate).astype(jnp.bfloat16)
    up_wgrad = apply_mask(contract_rows(normed, up_grad), mask_up).astype(jnp.bfloat16)
    normed_grad = contract_cols(gate_grad, eff_gate) + contract_cols(up_grad, eff_up)
    gain_grad = lax.optimization_barrier(jnp.sum(normed_grad * x_float * scale, axis=0))
    dots = lax.optimization_barrier(jnp.sum(normed_grad * norm_gain[None, :] * x_float, axis=1))[:, None]
    input_grad = (out_grad.astype(jnp.float32) + scale * norm_gain[None, :] * normed_grad - x_float * scale * scale * scale * dots / D).astype(jnp.bfloat16)
    return (layer_out, input_grad, gain_grad, gate_wgrad, up_wgrad, down_wgrad)
```

```python
import functools

import jax
import jax.numpy as jnp
from jax import lax
from jax.experimental import pallas as pl
from jax.experimental.pallas import tpu as pltpu
from jax.sharding import PartitionSpec as P

BLK = 128
LANES = 128
MESH = pl.DeviceIdType.MESH
F32 = jnp.float32
BF16 = jnp.bfloat16
norm_eps = 1e-05


def dot_nn(left, right):
    return lax.dot_general(left, right, (((1,), (0,)), ((), ())), preferred_element_type=F32)


def dot_nt(left, right):
    return lax.dot_general(left, right, (((1,), (1,)), ((), ())), preferred_element_type=F32)


def dot_tn(left, right):
    return lax.dot_general(left, right, (((0,), (0,)), ((), ())), preferred_element_type=F32)


W = 128


def layer_kernel(
    R, NZ, NX, G, total_width,
    x_ref, gain_ref, og_ref, mg_ref, mu_ref, md_ref, wg_hbm, wu_hbm, wd_hbm,
    out_ref, ig_ref, gg_out, agx_out, agz_out, nm_out, og_out,
    wg, wu, wd, nm_all, og_all, sq_mine, sq_all,
    xp, xr, xc, zp, zc, zx, agx, agz,
    acc_d, acc_n, fin_s, fin_r, gn_mine, gn_all, dt_mine, dt_all,
    w_sem, og_s, og_f, og_r, nm_s, nm_f, nm_r, sq_s, sq_r,
    x_s, x_r, xc_s, xc_r, zc_s, zc_r, zx_s, zx_r, axz_s, axz_r, axx_s, axx_r, az_s, az_r,
    fin_ss, fin_rs, gn_s, gn_r, dt_s, dt_r, out_s, tok_s,
):
    C = NZ * NX
    row = lax.axis_index("row")
    col = lax.axis_index("col")
    mz = col // NX
    mx = lax.rem(col, NX)
    rows, feats = x_ref.shape
    hidden = wg.shape[1]
    pairs = hidden // (2 * W)
    Q = G * pairs
    RG = R // G
    TG = RG * rows
    T = TG // (2 * NX)
    mine = row // RG
    low = mz == 0
    high = mz == NZ - 1
    end = jnp.logical_or(low, high)
    half = mz // (NZ - 1)
    far = jnp.maximum(mz, NZ - 1 - mz)

    def rpeer(k):
        return lax.rem(row + k, R)

    def cpeer(k):
        return lax.rem(col + k, C)

    def xpeer(k):
        return lax.rem(mx + k, NX)

    def group(g):
        return lax.rem(mine + 1 + g, G)

    other_core = row + 1 - 2 * lax.rem(row, 2)
    same_core = [lax.rem(row + 2 * k, R) for k in range(1, R // 2)]

    def remote(src, dst, ssem, rsem, dev):
        return pltpu.make_async_remote_copy(
            src_ref=src, dst_ref=dst, send_sem=ssem, recv_sem=rsem,
            device_id=dev, device_id_type=MESH,
        )

    def both(*conds):
        return functools.reduce(jnp.logical_and, conds)

    def live(q):
        return jnp.logical_and(q >= 0, q < Q)

    barrier = pltpu.get_barrier_semaphore()
    for k in range(1, R):
        pl.semaphore_signal(barrier, inc=1, device_id=(rpeer(k), col), device_id_type=MESH)
    for k in range(1, C):
        pl.semaphore_signal(barrier, inc=1, device_id=(row, cpeer(k)), device_id_type=MESH)
    loads = [
        pltpu.make_async_copy(src, dst, w_sem.at[i])
        for i, (src, dst) in enumerate(((wd_hbm, wd), (wg_hbm, wg), (wu_hbm, wu)))
    ]
    for load in loads:
        load.start()
    og_all[row] = og_ref[...]
    x = x_ref[...].astype(F32)
    tok = lax.broadcasted_iota(jnp.int32, (rows, LANES), 0)
    lane = lax.broadcasted_iota(jnp.int32, (rows, LANES), 1)
    diag = tok == lane

    def to_lanes(column):
        return jnp.sum(jnp.where(diag, column, 0.0), axis=0, keepdims=True)

    def to_column(line):
        return jnp.sum(jnp.where(diag, line, 0.0), axis=1, keepdims=True)

    sq_mine[...] = to_lanes(jnp.sum(x * x, axis=1, keepdims=True))
    sq_all[col] = sq_mine[...]
    pl.semaphore_wait(barrier, R - 1 + C - 1)

    def sq_copy(src, dev):
        return remote(sq_mine, sq_all.at[src], sq_s.at[dev], sq_r.at[src], (row, dev))

    for k in range(1, C):
        sq_copy(col, cpeer(k)).start()

    def tok_copy(kind, src, dev):
        blocks, ssem, _, rsem = kind
        return remote(blocks.at[src], blocks.at[src], ssem.at[dev], rsem.at[src], (dev, col))

    def tok_pass(kind, src):
        blocks, _, fsem, rsem = kind
        return remote(blocks.at[src], blocks.at[src], fsem.at[src], rsem.at[src], (other_core, col))

    og_kind = (og_all, og_s, og_f, og_r)
    nm_kind = (nm_all, nm_s, nm_f, nm_r)

    def tok_first(kind):
        for dev in same_core:
            tok_copy(kind, row, dev).start()
        tok_copy(kind, row, other_core).start()

    def tok_second(kind):
        for src in same_core:
            tok_copy(kind, src, src).wait_recv()
            tok_pass(kind, src).start()

    def tok_last(kind):
        for k in range(1, R):
            src = rpeer(k)

            @pl.when(lax.rem(src, 2) != lax.rem(row, 2))
            def _():
                tok_copy(kind, src, src).wait_recv()

    tok_first(og_kind)
    acc_d[...] = jnp.zeros_like(acc_d)
    acc_n[...] = jnp.zeros_like(acc_n)
    for k in range(1, C):
        sq_copy(cpeer(k), cpeer(k)).wait_recv()
    total = sq_all[0]
    for c in range(1, C):
        total = total + sq_all[c]
    scale = lax.rsqrt(to_column(total) / total_width + norm_eps)
    gain = gain_ref[...]
    nm_all[row] = (x * scale * gain).astype(BF16)
    tok_first(nm_kind)
    tok_second(og_kind)
    tok_second(nm_kind)

    def keep(mask_ref, r, c):
        return jnp.full((BLK, BLK), mask_ref[r, c].astype(F32), F32).astype(BF16)

    def columns(p):
        return pl.ds(pl.multiple_of(p * (2 * W), 2 * W), 2 * W)

    def mask_pair(p):
        per = 2 * W // BLK
        for b in range(per):
            at = pl.ds(pl.multiple_of(p * (2 * W) + b * BLK, BLK), BLK)
            block = p * per + b
            for r in range(feats // BLK):
                f = slice(r * BLK, (r + 1) * BLK)
                wd[at, f] = wd[at, f] * keep(md_ref, r, block)
                wg[f, at] = wg[f, at] * keep(mg_ref, r, block)
                wu[f, at] = wu[f, at] * keep(mu_ref, r, block)

    def parts(q):
        p = lax.rem(q, pairs)
        grp = group(q // pairs)
        cols = columns(p)

        @pl.when(q < pairs)
        def _():
            mask_pair(p)

        ogt = og_all[pl.ds(grp * RG, RG)].reshape(TG, feats)
        nmt = nm_all[pl.ds(grp * RG, RG)].reshape(TG, feats)
        for i in range(3):
            if i == 0:
                v = dot_nt(ogt, wd[cols, :])
            else:
                v = dot_nn(nmt, (wg, wu)[i - 1][:, cols])
            v = v.astype(BF16)
            for xx in range(NX):
                for h in range(2):
                    b = xx * 2 + h
                    xp[q, xx, h, i] = v[b * T : (b + 1) * T, :W]
            for h in range(2):
                zp[q, h, i] = v[h * NX * T : (h + 1) * NX * T, W:]

    def znb(step):
        return (row, (mz + step) * NX + mx)

    def x_copy(q, src, dev):
        return remote(
            xp.at[q, dev], xr.at[q, src], x_s.at[q, dev], x_r.at[q, src], (row, mz * NX + dev)
        )

    def xc_copy(q, h, step):
        return remote(xp.at[q, mx, h], xc.at[q, h], xc_s.at[q, h], xc_r.at[q, h], znb(step))

    def zc_copy(q, h, step):
        return remote(zp.at[q, h], zc.at[q, h], zc_s.at[q, h], zc_r.at[q, h], znb(step))

    def zx_copy(q, src, dev):
        return remote(
            zp.at[q, half], zx.at[q, src], zx_s.at[q, dev], zx_r.at[q, src], (row, mz * NX + dev)
        )

    def x_tokens(src, h):
        return pl.ds(pl.multiple_of((src * 2 + h) * T, T), T)

    def z_tokens(h):
        return pl.ds(pl.multiple_of(h * (NX * T), NX * T), NX * T)

    def axz_copy(q, h, step):
        block = agx.at[q, :, x_tokens(mx, h)]
        return remote(block, block, axz_s.at[q, h], axz_r.at[q, h], znb(step))

    def axx_copy(q, h, src, dev):
        block = agx.at[q, :, x_tokens(src, h)]
        return remote(
            block, block, axx_s.at[q, h, dev], axx_r.at[q, h, src], (row, mz * NX + dev)
        )

    def az_copy(q, h, step):
        block = agz.at[q, :, z_tokens(h)]
        return remote(block, block, az_s.at[q, h], az_r.at[q, h], znb(step))

    def pointwise(gate, up, da):
        sig = jax.nn.sigmoid(gate)
        return (
            (gate * sig * up).astype(BF16),
            (da * up * sig * (1.0 + gate * (1.0 - sig))).astype(BF16),
            (da * gate * sig).astype(BF16),
        )

    def x_send(q):
        @pl.when(live(q))
        def _():
            for k in range(1, NX):
                x_copy(q, mx, xpeer(k)).start()

    def share_x(q, h):
        for k in range(1, NX):
            axx_copy(q, h, mx, xpeer(k)).start()

    def spread_x():
        for h, step, hops in ((0, 1, mz), (1, -1, NZ - 1 - mz)):
            q = s_now[0] - NZ - hops

            @pl.when(both(live(q), hops > 0))
            def _():
                axz_copy(q, h, -step).wait_recv()

                @pl.when(hops < NZ - 1)
                def _():
                    axz_copy(q, h, step).start()

                share_x(q, h)

    def spread_z():
        for h, step, hops in ((0, 1, mz), (1, -1, NZ - 1 - mz)):
            q = s_now[0] - NZ - hops

            @pl.when(both(live(q), hops > 0))
            def _():
                az_copy(q, h, -step).wait_recv()

                @pl.when(hops < NZ - 1)
                def _():
                    az_copy(q, h, step).start()

    def chain_x():
        for h, step, hops in ((1, 1, mz), (0, -1, NZ - 1 - mz)):
            q = s_now[0] - 1 - hops

            @pl.when(both(live(q), hops > 0, hops < NZ - 1))
            def _():
                xc_copy(q, h, -step).wait_recv()
                xp[q, mx, h] = (xp[q, mx, h].astype(F32) + xc[q, h].astype(F32)).astype(BF16)
                xc_copy(q, h, step).start()

    def chain_z():
        for h, step, hops in ((1, 1, mz), (0, -1, NZ - 1 - mz)):
            q = s_now[0] - hops

            @pl.when(both(live(q), hops > 0, hops < NZ - 1))
            def _():
                zc_copy(q, h, -step).wait_recv()
                zp[q, h] = (zp[q, h].astype(F32) + zc[q, h].astype(F32)).astype(BF16)
                zc_copy(q, h, step).start()

    def sum_x(q):
        @pl.when(live(q))
        def _():
            for k in range(1, NX):
                x_copy(q, xpeer(k), xpeer(k)).wait_recv()
            for h in range(2):
                v = xp[q, mx, h].astype(F32)
                for k in range(1, NX):
                    v = v + xr[q, xpeer(k), h].astype(F32)
                xp[q, mx, h] = v.astype(BF16)

            @pl.when(low)
            def _():
                xc_copy(q, 1, 1).start()

            @pl.when(high)
            def _():
                xc_copy(q, 0, -1).start()

    def finish_x(q):
        for h, at_end, step in ((0, low, 1), (1, high, -1)):

            @pl.when(both(live(q), at_end))
            def _():
                xc_copy(q, h, step).wait_recv()
                da, gate, up = (
                    xp[q, mx, h, i].astype(F32) + xc[q, h, i].astype(F32) for i in range(3)
                )
                for i, v in enumerate(pointwise(gate, up, da)):
                    agx[q, i, x_tokens(mx, h)] = v
                axz_copy(q, h, step).start()
                share_x(q, h)

    def start_z(q):
        @pl.when(both(live(q), low))
        def _():
            zc_copy(q, 1, 1).start()

        @pl.when(both(live(q), high))
        def _():
            zc_copy(q, 0, -1).start()

    def exchange_z(q):
        for h, at_end, step in ((0, low, 1), (1, high, -1)):

            @pl.when(both(live(q), at_end))
            def _():
                zc_copy(q, h, step).wait_recv()
                zp[q, h] = (zp[q, h].astype(F32) + zc[q, h].astype(F32)).astype(BF16)
                for k in range(1, NX):
                    zx_copy(q, mx, xpeer(k)).start()

    def finish_z(q):
        for h, at_end, step in ((0, low, 1), (1, high, -1)):

            @pl.when(both(live(q), at_end))
            def _():
                for k in range(1, NX):
                    zx_copy(q, xpeer(k), xpeer(k)).wait_recv()

                def summed(i):
                    v = zp[q, h, i].astype(F32)
                    for k in range(1, NX):
                        v = v + zx[q, xpeer(k), i].astype(F32)
                    return v

                da, gate, up = (summed(i) for i in range(3))
                for i, v in enumerate(pointwise(gate, up, da)):
                    agz[q, i, h * NX * T : (h + 1) * NX * T] = v
                az_copy(q, h, step).start()

    def out_copies(q):
        return (
            pltpu.make_async_copy(agx.at[q], agx_out.at[q], out_s.at[q, 0]),
            pltpu.make_async_copy(agz.at[q], agz_out.at[q], out_s.at[q, 1]),
        )

    def products(q):
        @pl.when(live(q))
        def _():
            for h in range(2):
                for k in range(1, NX):
                    axx_copy(q, h, xpeer(k), xpeer(k)).wait_recv()
            for copy in out_copies(q):
                copy.start()
            grp = group(q // pairs)
            cols = columns(lax.rem(q, pairs))

            def tokens(i):
                return jnp.concatenate([agx[q, i], agz[q, i]], axis=1)

            acc_d[grp] += dot_nn(tokens(0), wd[cols, :])
            acc_n[grp] += dot_nt(tokens(1), wg[:, cols]) + dot_nt(tokens(2), wu[:, cols])

    def drain(q):
        @pl.when(live(q))
        def _():
            for k in range(1, NX):
                x_copy(q, mx, xpeer(k)).wait_send()
                for h in range(2):
                    axx_copy(q, h, mx, xpeer(k)).wait_send()
            for h, step, hops in ((1, 1, mz), (0, -1, NZ - 1 - mz)):

                @pl.when(hops < NZ - 1)
                def _():
                    xc_copy(q, h, step).wait_send()
                    zc_copy(q, h, step).wait_send()
                    axz_copy(q, 1 - h, step).wait_send()
                    az_copy(q, 1 - h, step).wait_send()

            @pl.when(end)
            def _():
                for k in range(1, NX):
                    zx_copy(q, mx, xpeer(k)).wait_send()

            for copy in out_copies(q):
                copy.wait()

    def fin_copy(src, dev):
        return remote(
            fin_s.at[dev], fin_r.at[src], fin_ss.at[dev], fin_rs.at[src], (dev, col)
        )

    def fin_rows(r):
        return pl.ds(pl.multiple_of(lax.rem(r, RG) * rows, rows), rows)

    def fin_send(r):
        fin_s[r, 0] = acc_d[r // RG, fin_rows(r)].astype(BF16)
        fin_s[r, 1] = acc_n[r // RG, fin_rows(r)].astype(BF16)
        fin_copy(row, r).start()

    for load in loads:
        load.wait()
    tok_last(og_kind)
    tok_last(nm_kind)
    nm_outs = [
        pltpu.make_async_copy(
            blocks.at[pl.ds(group(g) * RG, RG)], dst.at[pl.ds(g * RG, RG)], tok_s.at[i, g]
        )
        for i, (blocks, dst) in enumerate(((nm_all, nm_out), (og_all, og_out)))
        for g in range(G)
    ]
    for copy in nm_outs:
        copy.start()
    parts(0)
    s_now = [0]

    def one_step(s, carry):
        s_now[0] = s
        x_send(s)
        spread_x()
        chain_x()
        sum_x(s - 1)
        finish_x(s - NZ)

        @pl.when(s + 1 < Q)
        def _():
            parts(s + 1)

        start_z(s)
        spread_z()
        chain_z()
        exchange_z(s - (NZ - 1))
        finish_z(s - NZ)
        products(s - (NZ + 1 + far))
        drain(s - (2 * NZ + 2))
        for g in range(G - 1):

            @pl.when(s == (g + 1) * pairs - 1 + 2 * NZ)
            def _():
                for i in range(RG):
                    fin_send(group(g) * RG + i)

        return carry

    lax.fori_loop(0, Q + 2 * NZ, one_step, 0)

    for k in range(1, RG):
        fin_send(mine * RG + lax.rem(row + k, RG))
    for q in range(Q - 2, Q):
        drain(jnp.int32(q))
    for copy in nm_outs:
        copy.wait()
    for k in range(1, R):
        fin_copy(rpeer(k), rpeer(k)).wait_recv()
    down = acc_d[mine, fin_rows(row)]
    ngrad = acc_n[mine, fin_rows(row)]
    for k in range(1, R):
        down = down + fin_r[rpeer(k), 0].astype(F32)
        ngrad = ngrad + fin_r[rpeer(k), 1].astype(F32)
    x = x_ref[...].astype(F32)
    dt_mine[...] = to_lanes(jnp.sum(ngrad * gain * x, axis=1, keepdims=True))
    gn_mine[...] = jnp.sum(ngrad * x * scale, axis=0, keepdims=True)

    def dt_copy(src, dev):
        return remote(dt_mine, dt_all.at[src], dt_s.at[dev], dt_r.at[src], (row, dev))

    def gn_copy(src, dev):
        return remote(gn_mine, gn_all.at[src], gn_s.at[dev], gn_r.at[src], (dev, col))

    for k in range(1, C):
        dt_copy(col, cpeer(k)).start()
    for k in range(1, R):
        gn_copy(row, rpeer(k)).start()
    dt_all[col] = dt_mine[...]
    gn_all[row] = gn_mine[...]
    out_ref[...] = (x + down).astype(BF16)
    for dev in same_core:
        for kind in (og_kind, nm_kind):
            tok_copy(kind, row, dev).wait_send()
            tok_pass(kind, dev).wait_send()
    for kind in (og_kind, nm_kind):
        tok_copy(kind, row, other_core).wait_send()
    for k in range(1, R):
        fin_copy(row, rpeer(k)).wait_send()
    for k in range(1, C):
        sq_copy(col, cpeer(k)).wait_send()
    for k in range(1, C):
        dt_copy(cpeer(k), cpeer(k)).wait_recv()
    dots = dt_all[0]
    for c in range(1, C):
        dots = dots + dt_all[c]
    dots = to_column(dots)
    ig_ref[...] = (
        og_ref[...].astype(F32)
        + scale * gain * ngrad
        - x * scale * scale * scale * dots / total_width
    ).astype(BF16)
    for k in range(1, R):
        gn_copy(rpeer(k), rpeer(k)).wait_recv()
    gain_sum = gn_all[0]
    for r in range(1, R):
        gain_sum = gain_sum + gn_all[r]
    gg_out[...] = gain_sum
    for k in range(1, R):
        gn_copy(row, rpeer(k)).wait_send()
    for k in range(1, C):
        dt_copy(col, cpeer(k)).wait_send()


def wgrad_kernel(nm_ref, og_ref, agx_ref, agz_ref, mg_ref, mu_ref, md_ref,
                 lo_ref, ig_ref, gn_ref, gw_ref, uw_ref, dw_ref, lo_out, ig_out, gn_out):
    p = pl.program_id(0)

    @pl.when(p == 0)
    def _():
        lo_out[...] = lo_ref[...]
        ig_out[...] = ig_ref[...]
        gn_out[...] = gn_ref[...]

    G, _, _, TG, _ = agx_ref.shape
    feats = nm_ref.shape[1]
    per = 2 * W // BLK

    def tokens(i):
        return jnp.concatenate(
            [jnp.concatenate([agx_ref[g, 0, i], agz_ref[g, 0, i]], axis=1) for g in range(G)],
            axis=0,
        )

    for i, mask, dst in ((1, mg_ref, gw_ref), (2, mu_ref, uw_ref)):
        w = dot_tn(nm_ref[...], tokens(i))
        for r in range(feats // BLK):
            for b in range(per):
                at = (slice(r * BLK, (r + 1) * BLK), slice(b * BLK, (b + 1) * BLK))
                dst[at] = (w[at] * mask[r, p * per + b].astype(F32)).astype(BF16)
    w = dot_tn(tokens(0), og_ref[...])
    for r in range(feats // BLK):
        for b in range(per):
            at = (slice(b * BLK, (b + 1) * BLK), slice(r * BLK, (r + 1) * BLK))
            dw_ref[at] = (w[at] * md_ref[r, p * per + b].astype(F32)).astype(BF16)


def shards(R, C, layer_input, norm_gain, w_gate, w_up, w_down,
           mask_gate, mask_up, mask_down, out_grad):
    rows, feats = layer_input.shape
    hidden = w_gate.shape[1]
    tokens = rows * R
    NX = 1
    while (2 * NX) * (2 * NX) <= C:
        NX *= 2
    NZ = C // NX
    G = 2
    pairs = hidden // (2 * W)
    Q = G * pairs
    TG = tokens // G
    T = TG // (2 * NX)
    mask_down = mask_down.T
    vm = pl.BlockSpec(memory_space=pltpu.VMEM)
    sm = pl.BlockSpec(memory_space=pltpu.SMEM)
    hbm = pl.BlockSpec(memory_space=pl.ANY)
    dma = pltpu.SemaphoreType.DMA
    V = pltpu.VMEM
    out_shapes = (
        ((rows, feats), BF16), ((rows, feats), BF16), ((1, feats), F32),
        ((Q, 3, TG, W), BF16), ((Q, 3, TG, W), BF16),
        ((R, rows, feats), BF16), ((R, rows, feats), BF16),
    )
    scratch = [
        V((feats, hidden), BF16), V((feats, hidden), BF16), V((hidden, feats), BF16),
        V((R, rows, feats), BF16), V((R, rows, feats), BF16),
        V((1, LANES), F32), V((C, 1, LANES), F32),
        V((Q, NX, 2, 3, T, W), BF16), V((Q, NX, 2, 3, T, W), BF16), V((Q, 2, 3, T, W), BF16),
        V((Q, 2, 3, NX * T, W), BF16), V((Q, 2, 3, NX * T, W), BF16),
        V((Q, NX, 3, NX * T, W), BF16),
        V((Q, 3, TG, W), BF16), V((Q, 3, TG, W), BF16),
        V((G, TG, feats), F32), V((G, TG, feats), F32),
        V((R, 2, rows, feats), BF16), V((R, 2, rows, feats), BF16),
        V((1, feats), F32), V((R, 1, feats), F32),
        V((1, LANES), F32), V((C, 1, LANES), F32),
        dma((3,)),
        dma((R,)), dma((R,)), dma((R,)), dma((R,)), dma((R,)), dma((R,)),
        dma((C,)), dma((C,)),
        dma((Q, NX)), dma((Q, NX)), dma((Q, 2)), dma((Q, 2)), dma((Q, 2)), dma((Q, 2)),
        dma((Q, NX)), dma((Q, NX)), dma((Q, 2)), dma((Q, 2)),
        dma((Q, 2, NX)), dma((Q, 2, NX)), dma((Q, 2)), dma((Q, 2)),
        dma((R,)), dma((R,)), dma((R,)), dma((R,)), dma((C,)), dma((C,)),
        dma((Q, 2)), dma((2, G)),
    ]
    layer_out, input_grad, gain_grad, agx, agz, nm, og = pl.pallas_call(
        functools.partial(layer_kernel, R, NZ, NX, G, float(feats * C)),
        out_shape=tuple(jax.ShapeDtypeStruct(s, t) for s, t in out_shapes),
        in_specs=[vm] * 3 + [sm] * 3 + [hbm] * 3,
        out_specs=tuple([vm] * 3 + [hbm] * 4),
        scratch_shapes=scratch,
        compiler_params=pltpu.CompilerParams(
            collective_id=0, has_side_effects=True, vmem_limit_bytes=67043328
        ),
    )(layer_input, norm_gain[None, :], out_grad, mask_gate, mask_up, mask_down,
      w_gate, w_up, w_down)

    whole = lambda p: (0, 0)
    gate_wgrad, up_wgrad, down_wgrad, layer_out, input_grad, gain_grad = pl.pallas_call(
        wgrad_kernel,
        grid=(pairs,),
        out_shape=(
            jax.ShapeDtypeStruct((feats, hidden), BF16),
            jax.ShapeDtypeStruct((feats, hidden), BF16),
            jax.ShapeDtypeStruct((hidden, feats), BF16),
            jax.ShapeDtypeStruct((rows, feats), BF16),
            jax.ShapeDtypeStruct((rows, feats), BF16),
            jax.ShapeDtypeStruct((1, feats), F32),
        ),
        in_specs=[
            pl.BlockSpec((tokens, feats), whole),
            pl.BlockSpec((tokens, feats), whole),
            pl.BlockSpec((G, 1, 3, TG, W), lambda p: (0, p, 0, 0, 0)),
            pl.BlockSpec((G, 1, 3, TG, W), lambda p: (0, p, 0, 0, 0)),
            sm, sm, sm,
            pl.BlockSpec((rows, feats), whole),
            pl.BlockSpec((rows, feats), whole),
            pl.BlockSpec((1, feats), whole),
        ],
        out_specs=(
            pl.BlockSpec((feats, 2 * W), lambda p: (0, p)),
            pl.BlockSpec((feats, 2 * W), lambda p: (0, p)),
            pl.BlockSpec((2 * W, feats), lambda p: (p, 0)),
            pl.BlockSpec((rows, feats), whole),
            pl.BlockSpec((rows, feats), whole),
            pl.BlockSpec((1, feats), whole),
        ),
        compiler_params=pltpu.CompilerParams(vmem_limit_bytes=67043328),
    )(nm.reshape(tokens, feats), og.reshape(tokens, feats),
      agx.reshape(G, pairs, 3, TG, W), agz.reshape(G, pairs, 3, TG, W),
      mask_gate, mask_up, mask_down, layer_out, input_grad, gain_grad)
    return (layer_out, input_grad, gain_grad[0], gate_wgrad, up_wgrad, down_wgrad)


def solution(mesh):
    placed = (
        P("row", "col"),
        P("col"),
        P("col", "row"),
        P("col", "row"),
        P("row", "col"),
        P("col", "row"),
        P("col", "row"),
        P("row", "col"),
        P("row", "col"),
    )
    return jax.shard_map(
        functools.partial(shards, mesh.shape["row"], mesh.shape["col"]),
        mesh=mesh,
        in_specs=placed,
        out_specs=(
            P("row", "col"),
            P("row", "col"),
            P("col"),
            P("col", "row"),
            P("col", "row"),
            P("row", "col"),
        ),
        check_vma=False,
    )
```

```python
import functools

import jax
import jax.numpy as jnp
from jax import lax
from jax.experimental import pallas as pl
from jax.experimental.pallas import tpu as pltpu
from jax.sharding import PartitionSpec as P

BLK = 128
LANES = 128
MESH = pl.DeviceIdType.MESH
F32 = jnp.float32
BF16 = jnp.bfloat16
norm_eps = 1e-05


def dot_nn(left, right):
    return lax.dot_general(left, right, (((1,), (0,)), ((), ())), preferred_element_type=F32)


def dot_nt(left, right):
    return lax.dot_general(left, right, (((1,), (1,)), ((), ())), preferred_element_type=F32)


def dot_tn(left, right):
    return lax.dot_general(left, right, (((0,), (0,)), ((), ())), preferred_element_type=F32)


G = 2
W = 128
H = 2


def layer_kernel(
    R, NZ, NX, total_width,
    x_ref, gain_ref, og_ref, mg_ref, mu_ref, md_ref, wg_hbm, wu_hbm, wd_hbm,
    out_ref, ig_ref, gg_out, agx_out, agz_out, nm_out, og_out,
    wg, wu, wd, nm_all, og_all, sq_mine, sq_all,
    xp, xr, xc, zp, zc, zx, agx, agz,
    acc_d, acc_n, fin_s, fin_r, gn_mine, gn_all, dt_mine, dt_all,
    w_sem, og_s, og_f, og_r, nm_s, nm_f, nm_r, sq_s, sq_r,
    x_s, x_r, xc_s, xc_r, zc_s, zc_r, zx_s, zx_r, axz_s, axz_r, axx_s, axx_r, az_s, az_r,
    fin_ss, fin_rs, gn_s, gn_r, dt_s, dt_r, out_s, tok_s,
):
    C = NZ * NX
    row = lax.axis_index("row")
    col = lax.axis_index("col")
    mz = col // NX
    mx = lax.rem(col, NX)
    rows, feats = x_ref.shape
    hidden = wg.shape[1]
    pairs = hidden // (2 * W)
    Q = G * pairs
    RG = R // G
    TG = RG * rows
    T = TG // (2 * NX)
    mine = row // RG
    low = mz == 0
    high = mz == NZ - 1
    end = jnp.logical_or(low, high)
    half = mz // (NZ - 1)
    far = jnp.maximum(mz, NZ - 1 - mz)

    def rpeer(k):
        return lax.rem(row + k, R)

    def cpeer(k):
        return lax.rem(col + k, C)

    def xpeer(k):
        return lax.rem(mx + k, NX)

    first = (pairs + 1) // 2

    def place(q):
        return jnp.where(jnp.logical_or(q < first, q >= first + pairs), 1, 0)

    def pair(q):
        return jnp.where(q < first, q, jnp.where(q < first + pairs, q - first, q - pairs))

    def fresh(q):
        return jnp.logical_or(q < first, jnp.logical_and(q >= 2 * first, q < first + pairs))

    def group(place):
        return lax.rem(mine + 1 + place, G)

    other_core = row + 1 - 2 * lax.rem(row, 2)
    same_core = [lax.rem(row + 2 * k, R) for k in range(1, R // 2)]

    def remote(src, dst, ssem, rsem, dev):
        return pltpu.make_async_remote_copy(
            src_ref=src, dst_ref=dst, send_sem=ssem, recv_sem=rsem,
            device_id=dev, device_id_type=MESH,
        )

    def both(*conds):
        return functools.reduce(jnp.logical_and, conds)

    def live(q):
        return jnp.logical_and(q >= 0, q < Q)

    barrier = pltpu.get_barrier_semaphore()
    for k in range(1, R):
        pl.semaphore_signal(barrier, inc=1, device_id=(rpeer(k), col), device_id_type=MESH)
    for k in range(1, C):
        pl.semaphore_signal(barrier, inc=1, device_id=(row, cpeer(k)), device_id_type=MESH)
    loads = [
        pltpu.make_async_copy(src, dst, w_sem.at[i])
        for i, (src, dst) in enumerate(((wd_hbm, wd), (wg_hbm, wg), (wu_hbm, wu)))
    ]
    for load in loads:
        load.start()
    og_all[row] = og_ref[...]
    x = x_ref[...].astype(F32)
    tok = lax.broadcasted_iota(jnp.int32, (rows, LANES), 0)
    lane = lax.broadcasted_iota(jnp.int32, (rows, LANES), 1)
    diag = tok == lane

    def to_lanes(column):
        return jnp.sum(jnp.where(diag, column, 0.0), axis=0, keepdims=True)

    def to_column(line):
        return jnp.sum(jnp.where(diag, line, 0.0), axis=1, keepdims=True)

    sq_mine[...] = to_lanes(jnp.sum(x * x, axis=1, keepdims=True))
    sq_all[col] = sq_mine[...]
    pl.semaphore_wait(barrier, R - 1 + C - 1)

    def sq_copy(src, dev):
        return remote(sq_mine, sq_all.at[src], sq_s.at[dev], sq_r.at[src], (row, dev))

    for k in range(1, C):
        sq_copy(col, cpeer(k)).start()

    def tok_copy(kind, src, dev):
        blocks, ssem, _, rsem = kind
        return remote(blocks.at[src], blocks.at[src], ssem.at[dev], rsem.at[src], (dev, col))

    def tok_pass(kind, src):
        blocks, _, fsem, rsem = kind
        return remote(blocks.at[src], blocks.at[src], fsem.at[src], rsem.at[src], (other_core, col))

    og_kind = (og_all, og_s, og_f, og_r)
    nm_kind = (nm_all, nm_s, nm_f, nm_r)

    def tok_first(kind):
        tok_copy(kind, row, other_core).start()
        for dev in same_core:
            tok_copy(kind, row, dev).start()

    def tok_second(kind, own):
        for src in same_core:

            @pl.when((src // RG == mine) == own)
            def _():
                tok_copy(kind, src, src).wait_recv()
                tok_pass(kind, src).start()

    def tok_last(kind, own):
        for k in range(1, R):
            src = rpeer(k)

            @pl.when(
                jnp.logical_and(lax.rem(src, 2) != lax.rem(row, 2), (src // RG == mine) == own)
            )
            def _():
                tok_copy(kind, src, src).wait_recv()

    tok_first(og_kind)
    acc_d[...] = jnp.zeros_like(acc_d)
    acc_n[...] = jnp.zeros_like(acc_n)
    for k in range(1, C):
        sq_copy(cpeer(k), cpeer(k)).wait_recv()
    total = sq_all[0]
    for c in range(1, C):
        total = total + sq_all[c]
    scale = lax.rsqrt(to_column(total) / total_width + norm_eps)
    gain = gain_ref[...]
    nm_all[row] = (x * scale * gain).astype(BF16)
    tok_first(nm_kind)

    def keep(mask_ref, r, c):
        return jnp.full((BLK, BLK), mask_ref[r, c].astype(F32), F32).astype(BF16)

    def columns(p):
        return pl.ds(pl.multiple_of(p * (2 * W), 2 * W), 2 * W)

    def mask_pair(p):
        per = 2 * W // BLK
        for b in range(per):
            at = pl.ds(pl.multiple_of(p * (2 * W) + b * BLK, BLK), BLK)
            block = p * per + b
            for r in range(feats // BLK):
                f = slice(r * BLK, (r + 1) * BLK)
                wd[at, f] = wd[at, f] * keep(md_ref, r, block)
                wg[f, at] = wg[f, at] * keep(mg_ref, r, block)
                wu[f, at] = wu[f, at] * keep(mu_ref, r, block)

    def parts(q):
        p = pair(q)
        grp = group(place(q))
        cols = columns(p)

        @pl.when(fresh(q))
        def _():
            mask_pair(p)

        ogt = og_all[pl.ds(grp * RG, RG)].reshape(TG, feats)
        nmt = nm_all[pl.ds(grp * RG, RG)].reshape(TG, feats)
        for i in range(3):
            if i == 0:
                v = dot_nt(ogt, wd[cols, :])
            else:
                v = dot_nn(nmt, (wg, wu)[i - 1][:, cols])
            v = v.astype(BF16)
            for xx in range(NX):
                for h in range(2):
                    b = xx * 2 + h
                    xp[q, xx, h, i] = v[b * T : (b + 1) * T, :W]
            for h in range(2):
                zp[q, h, i] = v[h * NX * T : (h + 1) * NX * T, W:]

    def znb(step):
        return (row, (mz + step) * NX + mx)

    def x_copy(q, src, dev):
        return remote(
            xp.at[q, dev], xr.at[q, src], x_s.at[q, dev], x_r.at[q, src], (row, mz * NX + dev)
        )

    def xc_copy(q, h, step):
        return remote(xp.at[q, mx, h], xc.at[q, h], xc_s.at[q, h], xc_r.at[q, h], znb(step))

    def zc_copy(q, h, step):
        return remote(zp.at[q, h], zc.at[q, h], zc_s.at[q, h], zc_r.at[q, h], znb(step))

    def zx_copy(q, src, dev):
        return remote(
            zp.at[q, half], zx.at[q, src], zx_s.at[q, dev], zx_r.at[q, src], (row, mz * NX + dev)
        )

    def x_tokens(src, h):
        return pl.ds(pl.multiple_of((src * 2 + h) * T, T), T)

    def z_tokens(h):
        return pl.ds(pl.multiple_of(h * (NX * T), NX * T), NX * T)

    def axz_copy(q, h, step):
        block = agx.at[q, :, x_tokens(mx, h)]
        return remote(block, block, axz_s.at[q, h], axz_r.at[q, h], znb(step))

    def axx_copy(q, h, src, dev):
        block = agx.at[q, :, x_tokens(src, h)]
        return remote(
            block, block, axx_s.at[q, h, dev], axx_r.at[q, h, src], (row, mz * NX + dev)
        )

    def az_copy(q, h, step):
        block = agz.at[q, :, z_tokens(h)]
        return remote(block, block, az_s.at[q, h], az_r.at[q, h], znb(step))

    def pointwise(gate, up, da):
        sig = jax.nn.sigmoid(gate)
        return (
            (gate * sig * up).astype(BF16),
            (da * up * sig * (1.0 + gate * (1.0 - sig))).astype(BF16),
            (da * gate * sig).astype(BF16),
        )

    def x_send(q):
        @pl.when(live(q))
        def _():
            for k in range(1, NX):
                x_copy(q, mx, xpeer(k)).start()

    def share_x(q, h):
        for k in range(1, NX):
            axx_copy(q, h, mx, xpeer(k)).start()

    def spread_x():
        for h, step, hops in ((0, 1, mz), (1, -1, NZ - 1 - mz)):
            q = s_now[0] - H * (NZ + hops)

            @pl.when(both(live(q), hops > 0))
            def _():
                axz_copy(q, h, -step).wait_recv()

                @pl.when(hops < NZ - 1)
                def _():
                    axz_copy(q, h, step).start()

                share_x(q, h)

    def spread_z():
        for h, step, hops in ((0, 1, mz), (1, -1, NZ - 1 - mz)):
            q = s_now[0] - H * (NZ + hops)

            @pl.when(both(live(q), hops > 0))
            def _():
                az_copy(q, h, -step).wait_recv()

                @pl.when(hops < NZ - 1)
                def _():
                    az_copy(q, h, step).start()

    def chain_x():
        for h, step, hops in ((1, 1, mz), (0, -1, NZ - 1 - mz)):
            q = s_now[0] - H * (1 + hops)

            @pl.when(both(live(q), hops > 0, hops < NZ - 1))
            def _():
                xc_copy(q, h, -step).wait_recv()
                xp[q, mx, h] = (xp[q, mx, h].astype(F32) + xc[q, h].astype(F32)).astype(BF16)
                xc_copy(q, h, step).start()

    def chain_z():
        for h, step, hops in ((1, 1, mz), (0, -1, NZ - 1 - mz)):
            q = s_now[0] - H * hops

            @pl.when(both(live(q), hops > 0, hops < NZ - 1))
            def _():
                zc_copy(q, h, -step).wait_recv()
                zp[q, h] = (zp[q, h].astype(F32) + zc[q, h].astype(F32)).astype(BF16)
                zc_copy(q, h, step).start()

    def sum_x(q):
        @pl.when(live(q))
        def _():
            for k in range(1, NX):
                x_copy(q, xpeer(k), xpeer(k)).wait_recv()
            for h in range(2):
                v = xp[q, mx, h].astype(F32)
                for k in range(1, NX):
                    v = v + xr[q, xpeer(k), h].astype(F32)
                xp[q, mx, h] = v.astype(BF16)

            @pl.when(low)
            def _():
                xc_copy(q, 1, 1).start()

            @pl.when(high)
            def _():
                xc_copy(q, 0, -1).start()

    def finish_x(q):
        for h, at_end, step in ((0, low, 1), (1, high, -1)):

            @pl.when(both(live(q), at_end))
            def _():
                xc_copy(q, h, step).wait_recv()
                da, gate, up = (
                    xp[q, mx, h, i].astype(F32) + xc[q, h, i].astype(F32) for i in range(3)
                )
                for i, v in enumerate(pointwise(gate, up, da)):
                    agx[q, i, x_tokens(mx, h)] = v
                axz_copy(q, h, step).start()
                share_x(q, h)

    def start_z(q):
        @pl.when(both(live(q), low))
        def _():
            zc_copy(q, 1, 1).start()

        @pl.when(both(live(q), high))
        def _():
            zc_copy(q, 0, -1).start()

    def exchange_z(q):
        for h, at_end, step in ((0, low, 1), (1, high, -1)):

            @pl.when(both(live(q), at_end))
            def _():
                zc_copy(q, h, step).wait_recv()
                zp[q, h] = (zp[q, h].astype(F32) + zc[q, h].astype(F32)).astype(BF16)
                for k in range(1, NX):
                    zx_copy(q, mx, xpeer(k)).start()

    def finish_z(q):
        for h, at_end, step in ((0, low, 1), (1, high, -1)):

            @pl.when(both(live(q), at_end))
            def _():
                for k in range(1, NX):
                    zx_copy(q, xpeer(k), xpeer(k)).wait_recv()

                def summed(i):
                    v = zp[q, h, i].astype(F32)
                    for k in range(1, NX):
                        v = v + zx[q, xpeer(k), i].astype(F32)
                    return v

                da, gate, up = (summed(i) for i in range(3))
                for i, v in enumerate(pointwise(gate, up, da)):
                    agz[q, i, h * NX * T : (h + 1) * NX * T] = v
                az_copy(q, h, step).start()

    def out_copies(q):
        return (
            pltpu.make_async_copy(agx.at[q], agx_out.at[place(q), pair(q)], out_s.at[q, 0]),
            pltpu.make_async_copy(agz.at[q], agz_out.at[place(q), pair(q)], out_s.at[q, 1]),
        )

    def products(q):
        @pl.when(live(q))
        def _():
            for h in range(2):
                for k in range(1, NX):
                    axx_copy(q, h, xpeer(k), xpeer(k)).wait_recv()
            for copy in out_copies(q):
                copy.start()
            grp = group(place(q))
            cols = columns(pair(q))

            def tokens(i):
                return jnp.concatenate([agx[q, i], agz[q, i]], axis=1)

            acc_d[grp] += dot_nn(tokens(0), wd[cols, :])
            acc_n[grp] += dot_nt(tokens(1), wg[:, cols]) + dot_nt(tokens(2), wu[:, cols])

    def drain(q):
        @pl.when(live(q))
        def _():
            for k in range(1, NX):
                x_copy(q, mx, xpeer(k)).wait_send()
                for h in range(2):
                    axx_copy(q, h, mx, xpeer(k)).wait_send()
            for h, step, hops in ((1, 1, mz), (0, -1, NZ - 1 - mz)):

                @pl.when(hops < NZ - 1)
                def _():
                    xc_copy(q, h, step).wait_send()
                    zc_copy(q, h, step).wait_send()
                    axz_copy(q, 1 - h, step).wait_send()
                    az_copy(q, 1 - h, step).wait_send()

            @pl.when(end)
            def _():
                for k in range(1, NX):
                    zx_copy(q, mx, xpeer(k)).wait_send()

            for copy in out_copies(q):
                copy.wait()

    def fin_copy(src, dev):
        return remote(
            fin_s.at[dev], fin_r.at[src], fin_ss.at[dev], fin_rs.at[src], (dev, col)
        )

    def fin_rows(r):
        return pl.ds(pl.multiple_of(lax.rem(r, RG) * rows, rows), rows)

    def fin_send(r):
        fin_s[r, 0] = acc_d[r // RG, fin_rows(r)].astype(BF16)
        fin_s[r, 1] = acc_n[r // RG, fin_rows(r)].astype(BF16)
        fin_copy(row, r).start()

    for kind in (og_kind, nm_kind):
        tok_second(kind, True)
    for load in loads:
        load.wait()
    for kind in (og_kind, nm_kind):
        tok_last(kind, True)
    nm_outs = [
        pltpu.make_async_copy(
            blocks.at[pl.ds(group(g) * RG, RG)], dst.at[pl.ds(g * RG, RG)], tok_s.at[i, g]
        )
        for i, (blocks, dst) in enumerate(((nm_all, nm_out), (og_all, og_out)))
        for g in range(G)
    ]
    parts(0)
    s_now = [0]

    def one_step(s, carry):
        s_now[0] = s
        x_send(s)
        spread_x()
        chain_x()
        sum_x(s - H)
        finish_x(s - H * NZ)

        @pl.when(s == min(2, first - 1))
        def _():
            for kind in (og_kind, nm_kind):
                tok_second(kind, False)

        @pl.when(s == first - 1)
        def _():
            for kind in (og_kind, nm_kind):
                tok_last(kind, False)
            for copy in nm_outs:
                copy.start()

        @pl.when(s + 1 < Q)
        def _():
            parts(s + 1)

        start_z(s)
        spread_z()
        chain_z()
        exchange_z(s - H * (NZ - 1))
        finish_z(s - H * NZ)
        products(s - H * (NZ + 1 + far))
        drain(s - 2 * H * NZ - 2)

        @pl.when(s == first + pairs - 1 + 2 * H * NZ)
        def _():
            for i in range(RG):
                fin_send(group(0) * RG + i)

        return carry

    lax.fori_loop(0, Q + 2 * H * NZ, one_step, 0)

    for k in range(1, RG):
        fin_send(mine * RG + lax.rem(row + k, RG))
    for q in range(Q - 2, Q):
        drain(jnp.int32(q))
    for copy in nm_outs:
        copy.wait()
    for k in range(1, R):
        fin_copy(rpeer(k), rpeer(k)).wait_recv()
    down = acc_d[mine, fin_rows(row)]
    ngrad = acc_n[mine, fin_rows(row)]
    for k in range(1, R):
        down = down + fin_r[rpeer(k), 0].astype(F32)
        ngrad = ngrad + fin_r[rpeer(k), 1].astype(F32)
    x = x_ref[...].astype(F32)
    dt_mine[...] = to_lanes(jnp.sum(ngrad * gain * x, axis=1, keepdims=True))
    gn_mine[...] = jnp.sum(ngrad * x * scale, axis=0, keepdims=True)

    def dt_copy(src, dev):
        return remote(dt_mine, dt_all.at[src], dt_s.at[dev], dt_r.at[src], (row, dev))

    def gn_copy(src, dev):
        return remote(gn_mine, gn_all.at[src], gn_s.at[dev], gn_r.at[src], (dev, col))

    for k in range(1, C):
        dt_copy(col, cpeer(k)).start()
    for k in range(1, R):
        gn_copy(row, rpeer(k)).start()
    dt_all[col] = dt_mine[...]
    gn_all[row] = gn_mine[...]
    out_ref[...] = (x + down).astype(BF16)
    for dev in same_core:
        for kind in (og_kind, nm_kind):
            tok_copy(kind, row, dev).wait_send()
            tok_pass(kind, dev).wait_send()
    for kind in (og_kind, nm_kind):
        tok_copy(kind, row, other_core).wait_send()
    for k in range(1, R):
        fin_copy(row, rpeer(k)).wait_send()
    for k in range(1, C):
        sq_copy(col, cpeer(k)).wait_send()
    for k in range(1, C):
        dt_copy(cpeer(k), cpeer(k)).wait_recv()
    dots = dt_all[0]
    for c in range(1, C):
        dots = dots + dt_all[c]
    dots = to_column(dots)
    ig_ref[...] = (
        og_ref[...].astype(F32)
        + scale * gain * ngrad
        - x * scale * scale * scale * dots / total_width
    ).astype(BF16)
    for k in range(1, R):
        gn_copy(rpeer(k), rpeer(k)).wait_recv()
    gain_sum = gn_all[0]
    for r in range(1, R):
        gain_sum = gain_sum + gn_all[r]
    gg_out[...] = gain_sum
    for k in range(1, R):
        gn_copy(row, rpeer(k)).wait_send()
    for k in range(1, C):
        dt_copy(col, cpeer(k)).wait_send()


def wgrad_kernel(nm_ref, og_ref, agx_ref, agz_ref, mg_ref, mu_ref, md_ref,
                 lo_ref, ig_ref, gn_ref, gw_ref, uw_ref, dw_ref, lo_out, ig_out, gn_out):
    p = pl.program_id(0)

    @pl.when(p == 0)
    def _():
        lo_out[...] = lo_ref[...]
        ig_out[...] = ig_ref[...]
        gn_out[...] = gn_ref[...]

    step = agx_ref.shape[1]
    feats = nm_ref.shape[1]
    per = step * 2 * W // BLK

    def tokens(i):
        return jnp.concatenate(
            [
                jnp.concatenate([ref[g, k, i] for k in range(step) for ref in (agx_ref, agz_ref)], axis=1)
                for g in range(G)
            ],
            axis=0,
        )

    for i, mask, dst in ((1, mg_ref, gw_ref), (2, mu_ref, uw_ref)):
        w = dot_tn(nm_ref[...], tokens(i))
        for r in range(feats // BLK):
            for b in range(per):
                at = (slice(r * BLK, (r + 1) * BLK), slice(b * BLK, (b + 1) * BLK))
                dst[at] = (w[at] * mask[r, p * per + b].astype(F32)).astype(BF16)
    w = dot_tn(tokens(0), og_ref[...])
    for r in range(feats // BLK):
        for b in range(per):
            at = (slice(b * BLK, (b + 1) * BLK), slice(r * BLK, (r + 1) * BLK))
            dw_ref[at] = (w[at] * md_ref[r, p * per + b].astype(F32)).astype(BF16)


def shards(R, C, layer_input, norm_gain, w_gate, w_up, w_down,
           mask_gate, mask_up, mask_down, out_grad):
    rows, feats = layer_input.shape
    hidden = w_gate.shape[1]
    tokens = rows * R
    NX = 1
    while (2 * NX) * (2 * NX) <= C:
        NX *= 2
    NZ = C // NX
    pairs = hidden // (2 * W)
    Q = G * pairs
    TG = tokens // G
    T = TG // (2 * NX)
    mask_down = mask_down.T
    vm = pl.BlockSpec(memory_space=pltpu.VMEM)
    sm = pl.BlockSpec(memory_space=pltpu.SMEM)
    hbm = pl.BlockSpec(memory_space=pl.ANY)
    dma = pltpu.SemaphoreType.DMA
    V = pltpu.VMEM
    out_shapes = (
        ((rows, feats), BF16), ((rows, feats), BF16), ((1, feats), F32),
        ((G, pairs, 3, TG, W), BF16), ((G, pairs, 3, TG, W), BF16),
        ((R, rows, feats), BF16), ((R, rows, feats), BF16),
    )
    scratch = [
        V((feats, hidden), BF16), V((feats, hidden), BF16), V((hidden, feats), BF16),
        V((R, rows, feats), BF16), V((R, rows, feats), BF16),
        V((1, LANES), F32), V((C, 1, LANES), F32),
        V((Q, NX, 2, 3, T, W), BF16), V((Q, NX, 2, 3, T, W), BF16), V((Q, 2, 3, T, W), BF16),
        V((Q, 2, 3, NX * T, W), BF16), V((Q, 2, 3, NX * T, W), BF16),
        V((Q, NX, 3, NX * T, W), BF16),
        V((Q, 3, TG, W), BF16), V((Q, 3, TG, W), BF16),
        V((G, TG, feats), F32), V((G, TG, feats), F32),
        V((R, 2, rows, feats), BF16), V((R, 2, rows, feats), BF16),
        V((1, feats), F32), V((R, 1, feats), F32),
        V((1, LANES), F32), V((C, 1, LANES), F32),
        dma((3,)),
        dma((R,)), dma((R,)), dma((R,)), dma((R,)), dma((R,)), dma((R,)),
        dma((C,)), dma((C,)),
        dma((Q, NX)), dma((Q, NX)), dma((Q, 2)), dma((Q, 2)), dma((Q, 2)), dma((Q, 2)),
        dma((Q, NX)), dma((Q, NX)), dma((Q, 2)), dma((Q, 2)),
        dma((Q, 2, NX)), dma((Q, 2, NX)), dma((Q, 2)), dma((Q, 2)),
        dma((R,)), dma((R,)), dma((R,)), dma((R,)), dma((C,)), dma((C,)),
        dma((Q, 2)), dma((2, G)),
    ]
    layer_out, input_grad, gain_grad, agx, agz, nm, og = pl.pallas_call(
        functools.partial(layer_kernel, R, NZ, NX, float(feats * C)),
        out_shape=tuple(jax.ShapeDtypeStruct(s, t) for s, t in out_shapes),
        in_specs=[vm] * 3 + [sm] * 3 + [hbm] * 3,
        out_specs=tuple([vm] * 3 + [hbm] * 4),
        scratch_shapes=scratch,
        compiler_params=pltpu.CompilerParams(
            collective_id=0, has_side_effects=True, vmem_limit_bytes=67043328
        ),
    )(layer_input, norm_gain[None, :], out_grad, mask_gate, mask_up, mask_down,
      w_gate, w_up, w_down)

    whole = lambda p: (0, 0)
    step = 2 if pairs % 2 == 0 else 1
    gate_wgrad, up_wgrad, down_wgrad, layer_out, input_grad, gain_grad = pl.pallas_call(
        wgrad_kernel,
        grid=(pairs // step,),
        out_shape=(
            jax.ShapeDtypeStruct((feats, hidden), BF16),
            jax.ShapeDtypeStruct((feats, hidden), BF16),
            jax.ShapeDtypeStruct((hidden, feats), BF16),
            jax.ShapeDtypeStruct((rows, feats), BF16),
            jax.ShapeDtypeStruct((rows, feats), BF16),
            jax.ShapeDtypeStruct((1, feats), F32),
        ),
        in_specs=[
            pl.BlockSpec((tokens, feats), whole),
            pl.BlockSpec((tokens, feats), whole),
            pl.BlockSpec((G, step, 3, TG, W), lambda p: (0, p, 0, 0, 0)),
            pl.BlockSpec((G, step, 3, TG, W), lambda p: (0, p, 0, 0, 0)),
            sm, sm, sm,
            pl.BlockSpec((rows, feats), whole),
            pl.BlockSpec((rows, feats), whole),
            pl.BlockSpec((1, feats), whole),
        ],
        out_specs=(
            pl.BlockSpec((feats, step * 2 * W), lambda p: (0, p)),
            pl.BlockSpec((feats, step * 2 * W), lambda p: (0, p)),
            pl.BlockSpec((step * 2 * W, feats), lambda p: (p, 0)),
            pl.BlockSpec((rows, feats), whole),
            pl.BlockSpec((rows, feats), whole),
            pl.BlockSpec((1, feats), whole),
        ),
        compiler_params=pltpu.CompilerParams(vmem_limit_bytes=67043328),
    )(nm.reshape(tokens, feats), og.reshape(tokens, feats),
      agx, agz,
      mask_gate, mask_up, mask_down, layer_out, input_grad, gain_grad)
    return (layer_out, input_grad, gain_grad[0], gate_wgrad, up_wgrad, down_wgrad)


def solution(mesh):
    placed = (
        P("row", "col"),
        P("col"),
        P("col", "row"),
        P("col", "row"),
        P("row", "col"),
        P("col", "row"),
        P("col", "row"),
        P("row", "col"),
        P("row", "col"),
    )
    return jax.shard_map(
        functools.partial(shards, mesh.shape["row"], mesh.shape["col"]),
        mesh=mesh,
        in_specs=placed,
        out_specs=(
            P("row", "col"),
            P("row", "col"),
            P("col"),
            P("col", "row"),
            P("col", "row"),
            P("row", "col"),
        ),
        check_vma=False,
    )
```

```python
import functools

import jax
import jax.numpy as jnp
from jax import lax
from jax.experimental import pallas as pl
from jax.experimental.pallas import tpu as pltpu
from jax.sharding import PartitionSpec as P

BLK = 128
LANES = 128
MESH = pl.DeviceIdType.MESH
F32 = jnp.float32
BF16 = jnp.bfloat16
norm_eps = 1e-05


def dot_nn(left, right):
    return lax.dot_general(left, right, (((1,), (0,)), ((), ())), preferred_element_type=F32)


def dot_nt(left, right):
    return lax.dot_general(left, right, (((1,), (1,)), ((), ())), preferred_element_type=F32)


def dot_tn(left, right):
    return lax.dot_general(left, right, (((0,), (0,)), ((), ())), preferred_element_type=F32)


G = 2
W = 128
H = 2


DS = 4


def ring(Q, NZ):
    return min(Q, H * NZ + 2)


def layer_kernel(
    R, NZ, NX, total_width,
    x_ref, gain_ref, og_ref, mg_ref, mu_ref, md_ref, wg_hbm, wu_hbm, wd_hbm,
    out_ref, ig_ref, gg_out, agx_out, agz_out, nm_out, og_out,
    wg, wu, wd, nm_all, og_all, sq_mine, sq_all,
    xp, xr, xc, zp, zc, zx, agx, agz,
    acc_d, acc_n, fin_s, fin_r, gn_mine, gn_all, dt_mine, dt_all,
    w_sem, og_s, og_f, og_r, nm_s, nm_f, nm_r, sq_s, sq_r,
    x_s, x_r, xc_s, xc_r, zc_s, zc_r, zx_s, zx_r, axz_s, axz_r, axx_s, axx_r, az_s, az_r,
    fin_ss, fin_rs, gn_s, gn_r, dt_s, dt_r, out_s, tok_s,
):
    C = NZ * NX
    row = lax.axis_index("row")
    col = lax.axis_index("col")
    mz = col // NX
    mx = lax.rem(col, NX)
    rows, feats = x_ref.shape
    hidden = wg.shape[1]
    pairs = hidden // (2 * W)
    Q = G * pairs
    D = ring(Q, NZ)
    RG = R // G
    TG = RG * rows
    T = TG // (2 * NX)
    mine = row // RG
    low = mz == 0
    high = mz == NZ - 1
    end = jnp.logical_or(low, high)
    half = mz // (NZ - 1)
    far = jnp.maximum(mz, NZ - 1 - mz)

    def rpeer(k):
        return lax.rem(row + k, R)

    def cpeer(k):
        return lax.rem(col + k, C)

    def xpeer(k):
        return lax.rem(mx + k, NX)

    first = (pairs + 1) // 2

    def place(q):
        return jnp.where(jnp.logical_or(q < first, q >= first + pairs), 1, 0)

    def pair(q):
        return jnp.where(q < first, q, jnp.where(q < first + pairs, q - first, q - pairs))

    def fresh(q):
        return jnp.logical_or(q < first, jnp.logical_and(q >= 2 * first, q < first + pairs))

    def group(place):
        return lax.rem(mine + 1 + place, G)

    other_core = row + 1 - 2 * lax.rem(row, 2)
    same_core = [lax.rem(row + 2 * k, R) for k in range(1, R // 2)]

    def remote(src, dst, ssem, rsem, dev):
        return pltpu.make_async_remote_copy(
            src_ref=src, dst_ref=dst, send_sem=ssem, recv_sem=rsem,
            device_id=dev, device_id_type=MESH,
        )

    def both(*conds):
        return functools.reduce(jnp.logical_and, conds)

    def at_s(q):
        return lax.rem(q, DS)

    def at_r(q):
        return lax.rem(q, D)

    def send(make, q):
        @pl.when(q >= DS)
        def _():
            make(q - DS).wait_send()

        make(q).start()

    def live(q):
        return jnp.logical_and(q >= 0, q < Q)

    barrier = pltpu.get_barrier_semaphore()
    for k in range(1, R):
        pl.semaphore_signal(barrier, inc=1, device_id=(rpeer(k), col), device_id_type=MESH)
    for k in range(1, C):
        pl.semaphore_signal(barrier, inc=1, device_id=(row, cpeer(k)), device_id_type=MESH)
    loads = [
        pltpu.make_async_copy(src, dst, w_sem.at[i])
        for i, (src, dst) in enumerate(((wd_hbm, wd), (wg_hbm, wg), (wu_hbm, wu)))
    ]
    for load in loads:
        load.start()
    og_all[row] = og_ref[...]
    x = x_ref[...].astype(F32)
    tok = lax.broadcasted_iota(jnp.int32, (rows, LANES), 0)
    lane = lax.broadcasted_iota(jnp.int32, (rows, LANES), 1)
    diag = tok == lane

    def to_lanes(column):
        return jnp.sum(jnp.where(diag, column, 0.0), axis=0, keepdims=True)

    def to_column(line):
        return jnp.sum(jnp.where(diag, line, 0.0), axis=1, keepdims=True)

    sq_mine[...] = to_lanes(jnp.sum(x * x, axis=1, keepdims=True))
    sq_all[col] = sq_mine[...]
    pl.semaphore_wait(barrier, R - 1 + C - 1)

    def sq_copy(src, dev):
        return remote(sq_mine, sq_all.at[src], sq_s.at[dev], sq_r.at[src], (row, dev))

    for k in range(1, C):
        sq_copy(col, cpeer(k)).start()

    def tok_copy(kind, src, dev):
        blocks, ssem, _, rsem = kind
        return remote(blocks.at[src], blocks.at[src], ssem.at[dev], rsem.at[src], (dev, col))

    def tok_pass(kind, src):
        blocks, _, fsem, rsem = kind
        return remote(blocks.at[src], blocks.at[src], fsem.at[src], rsem.at[src], (other_core, col))

    og_kind = (og_all, og_s, og_f, og_r)
    nm_kind = (nm_all, nm_s, nm_f, nm_r)

    def tok_first(kind):
        tok_copy(kind, row, other_core).start()
        for dev in same_core:
            tok_copy(kind, row, dev).start()

    def tok_second(kind, own):
        for src in same_core:

            @pl.when((src // RG == mine) == own)
            def _():
                tok_copy(kind, src, src).wait_recv()
                tok_pass(kind, src).start()

    def tok_last(kind, own):
        for k in range(1, R):
            src = rpeer(k)

            @pl.when(
                jnp.logical_and(lax.rem(src, 2) != lax.rem(row, 2), (src // RG == mine) == own)
            )
            def _():
                tok_copy(kind, src, src).wait_recv()

    tok_first(og_kind)
    acc_d[...] = jnp.zeros_like(acc_d)
    acc_n[...] = jnp.zeros_like(acc_n)
    for k in range(1, C):
        sq_copy(cpeer(k), cpeer(k)).wait_recv()
    total = sq_all[0]
    for c in range(1, C):
        total = total + sq_all[c]
    scale = lax.rsqrt(to_column(total) / total_width + norm_eps)
    gain = gain_ref[...]
    nm_all[row] = (x * scale * gain).astype(BF16)
    tok_first(nm_kind)

    def keep(mask_ref, r, c):
        return jnp.full((BLK, BLK), mask_ref[r, c].astype(F32), F32).astype(BF16)

    def columns(p):
        return pl.ds(pl.multiple_of(p * (2 * W), 2 * W), 2 * W)

    def mask_pair(p):
        per = 2 * W // BLK
        for b in range(per):
            at = pl.ds(pl.multiple_of(p * (2 * W) + b * BLK, BLK), BLK)
            block = p * per + b
            for r in range(feats // BLK):
                f = slice(r * BLK, (r + 1) * BLK)
                wd[at, f] = wd[at, f] * keep(md_ref, r, block)
                wg[f, at] = wg[f, at] * keep(mg_ref, r, block)
                wu[f, at] = wu[f, at] * keep(mu_ref, r, block)

    def parts(q):
        p = pair(q)
        grp = group(place(q))
        cols = columns(p)

        @pl.when(fresh(q))
        def _():
            mask_pair(p)

        ogt = og_all[pl.ds(grp * RG, RG)].reshape(TG, feats)
        nmt = nm_all[pl.ds(grp * RG, RG)].reshape(TG, feats)
        for i in range(3):
            if i == 0:
                v = dot_nt(ogt, wd[cols, :])
            else:
                v = dot_nn(nmt, (wg, wu)[i - 1][:, cols])
            v = v.astype(BF16)
            for xx in range(NX):
                for h in range(2):
                    b = xx * 2 + h
                    xp[q, xx, h, i] = v[b * T : (b + 1) * T, :W]
            for h in range(2):
                zp[q, h, i] = v[h * NX * T : (h + 1) * NX * T, W:]

    def znb(step):
        return (row, (mz + step) * NX + mx)

    def x_copy(q, src, dev):
        return remote(
            xp.at[q, dev], xr.at[q, src], x_s.at[at_s(q), dev], x_r.at[at_r(q), src], (row, mz * NX + dev)
        )

    def xc_copy(q, h, step):
        return remote(
            xp.at[q, mx, h], xc.at[q, h], xc_s.at[at_s(q), h], xc_r.at[at_r(q), h], znb(step)
        )

    def zc_copy(q, h, step):
        return remote(
            zp.at[q, h], zc.at[q, h], zc_s.at[at_s(q), h], zc_r.at[at_r(q), h], znb(step)
        )

    def zx_copy(q, src, dev):
        return remote(
            zp.at[q, half], zx.at[q, src], zx_s.at[at_s(q), dev], zx_r.at[at_r(q), src],
            (row, mz * NX + dev),
        )

    def x_tokens(src, h):
        return pl.ds(pl.multiple_of((src * 2 + h) * T, T), T)

    def z_tokens(h):
        return pl.ds(pl.multiple_of(h * (NX * T), NX * T), NX * T)

    def axz_copy(q, h, step):
        block = agx.at[q, :, x_tokens(mx, h)]
        return remote(block, block, axz_s.at[at_s(q), h], axz_r.at[at_r(q), h], znb(step))

    def axx_copy(q, h, src, dev):
        block = agx.at[q, :, x_tokens(src, h)]
        return remote(
            block, block, axx_s.at[at_s(q), h, dev], axx_r.at[at_r(q), h, src],
            (row, mz * NX + dev),
        )

    def az_copy(q, h, step):
        block = agz.at[q, :, z_tokens(h)]
        return remote(block, block, az_s.at[at_s(q), h], az_r.at[at_r(q), h], znb(step))

    def pointwise(gate, up, da):
        sig = jax.nn.sigmoid(gate)
        return (
            (gate * sig * up).astype(BF16),
            (da * up * sig * (1.0 + gate * (1.0 - sig))).astype(BF16),
            (da * gate * sig).astype(BF16),
        )

    def x_send(q):
        @pl.when(live(q))
        def _():
            for k in range(1, NX):
                send(lambda q: x_copy(q, mx, xpeer(k)), q)

    def share_x(q, h):
        for k in range(1, NX):
            send(lambda q: axx_copy(q, h, mx, xpeer(k)), q)

    def spread_x():
        for h, step, hops in ((0, 1, mz), (1, -1, NZ - 1 - mz)):
            q = s_now[0] - H * (NZ + hops)

            @pl.when(both(live(q), hops > 0))
            def _():
                axz_copy(q, h, -step).wait_recv()

                @pl.when(hops < NZ - 1)
                def _():
                    send(lambda q: axz_copy(q, h, step), q)

                share_x(q, h)

    def spread_z():
        for h, step, hops in ((0, 1, mz), (1, -1, NZ - 1 - mz)):
            q = s_now[0] - H * (NZ + hops)

            @pl.when(both(live(q), hops > 0))
            def _():
                az_copy(q, h, -step).wait_recv()

                @pl.when(hops < NZ - 1)
                def _():
                    send(lambda q: az_copy(q, h, step), q)

    def chain_x():
        for h, step, hops in ((1, 1, mz), (0, -1, NZ - 1 - mz)):
            q = s_now[0] - H * (1 + hops)

            @pl.when(both(live(q), hops > 0, hops < NZ - 1))
            def _():
                xc_copy(q, h, -step).wait_recv()
                xp[q, mx, h] = (xp[q, mx, h].astype(F32) + xc[q, h].astype(F32)).astype(BF16)
                send(lambda q: xc_copy(q, h, step), q)

    def chain_z():
        for h, step, hops in ((1, 1, mz), (0, -1, NZ - 1 - mz)):
            q = s_now[0] - H * hops

            @pl.when(both(live(q), hops > 0, hops < NZ - 1))
            def _():
                zc_copy(q, h, -step).wait_recv()
                zp[q, h] = (zp[q, h].astype(F32) + zc[q, h].astype(F32)).astype(BF16)
                send(lambda q: zc_copy(q, h, step), q)

    def sum_x(q):
        @pl.when(live(q))
        def _():
            for k in range(1, NX):
                x_copy(q, xpeer(k), xpeer(k)).wait_recv()
            for h in range(2):
                v = xp[q, mx, h].astype(F32)
                for k in range(1, NX):
                    v = v + xr[q, xpeer(k), h].astype(F32)
                xp[q, mx, h] = v.astype(BF16)

            @pl.when(low)
            def _():
                send(lambda q: xc_copy(q, 1, 1), q)

            @pl.when(high)
            def _():
                send(lambda q: xc_copy(q, 0, -1), q)

    def finish_x(q):
        for h, at_end, step in ((0, low, 1), (1, high, -1)):

            @pl.when(both(live(q), at_end))
            def _():
                xc_copy(q, h, step).wait_recv()
                da, gate, up = (
                    xp[q, mx, h, i].astype(F32) + xc[q, h, i].astype(F32) for i in range(3)
                )
                for i, v in enumerate(pointwise(gate, up, da)):
                    agx[q, i, x_tokens(mx, h)] = v
                send(lambda q: axz_copy(q, h, step), q)
                share_x(q, h)

    def start_z(q):
        @pl.when(both(live(q), low))
        def _():
            send(lambda q: zc_copy(q, 1, 1), q)

        @pl.when(both(live(q), high))
        def _():
            send(lambda q: zc_copy(q, 0, -1), q)

    def exchange_z(q):
        for h, at_end, step in ((0, low, 1), (1, high, -1)):

            @pl.when(both(live(q), at_end))
            def _():
                zc_copy(q, h, step).wait_recv()
                zp[q, h] = (zp[q, h].astype(F32) + zc[q, h].astype(F32)).astype(BF16)
                for k in range(1, NX):
                    send(lambda q: zx_copy(q, mx, xpeer(k)), q)

    def finish_z(q):
        for h, at_end, step in ((0, low, 1), (1, high, -1)):

            @pl.when(both(live(q), at_end))
            def _():
                for k in range(1, NX):
                    zx_copy(q, xpeer(k), xpeer(k)).wait_recv()

                def summed(i):
                    v = zp[q, h, i].astype(F32)
                    for k in range(1, NX):
                        v = v + zx[q, xpeer(k), i].astype(F32)
                    return v

                da, gate, up = (summed(i) for i in range(3))
                for i, v in enumerate(pointwise(gate, up, da)):
                    agz[q, i, h * NX * T : (h + 1) * NX * T] = v
                send(lambda q: az_copy(q, h, step), q)

    def gather_x():
        for h, hops in ((0, mz), (1, NZ - 1 - mz)):
            q = s_now[0] - H * (NZ + 1 + hops)

            @pl.when(live(q))
            def _():
                for k in range(1, NX):
                    axx_copy(q, h, xpeer(k), xpeer(k)).wait_recv()

    def out_copies(q):
        return (
            pltpu.make_async_copy(agx.at[q], agx_out.at[place(q), pair(q)], out_s.at[at_s(q), 0]),
            pltpu.make_async_copy(agz.at[q], agz_out.at[place(q), pair(q)], out_s.at[at_s(q), 1]),
        )

    def products(q):
        @pl.when(live(q))
        def _():
            @pl.when(q >= DS)
            def _():
                for copy in out_copies(q - DS):
                    copy.wait()

            for copy in out_copies(q):
                copy.start()
            grp = group(place(q))
            cols = columns(pair(q))

            def tokens(i):
                return jnp.concatenate([agx[q, i], agz[q, i]], axis=1)

            acc_d[grp] += dot_nn(tokens(0), wd[cols, :])
            acc_n[grp] += dot_nt(tokens(1), wg[:, cols]) + dot_nt(tokens(2), wu[:, cols])

    def drain(q):
        for k in range(1, NX):
            x_copy(q, mx, xpeer(k)).wait_send()
            for h in range(2):
                axx_copy(q, h, mx, xpeer(k)).wait_send()
        for h, step, hops in ((1, 1, mz), (0, -1, NZ - 1 - mz)):

            @pl.when(hops < NZ - 1)
            def _():
                xc_copy(q, h, step).wait_send()
                zc_copy(q, h, step).wait_send()
                axz_copy(q, 1 - h, step).wait_send()
                az_copy(q, 1 - h, step).wait_send()

        @pl.when(end)
        def _():
            for k in range(1, NX):
                zx_copy(q, mx, xpeer(k)).wait_send()

        for copy in out_copies(q):
            copy.wait()

    def fin_copy(src, dev):
        return remote(
            fin_s.at[dev], fin_r.at[src], fin_ss.at[dev], fin_rs.at[src], (dev, col)
        )

    def fin_rows(r):
        return pl.ds(pl.multiple_of(lax.rem(r, RG) * rows, rows), rows)

    def fin_send(r):
        fin_s[r, 0] = acc_d[r // RG, fin_rows(r)].astype(BF16)
        fin_s[r, 1] = acc_n[r // RG, fin_rows(r)].astype(BF16)
        fin_copy(row, r).start()

    for kind in (og_kind, nm_kind):
        tok_second(kind, True)
    for load in loads:
        load.wait()
    for kind in (og_kind, nm_kind):
        tok_last(kind, True)
    nm_outs = [
        pltpu.make_async_copy(
            blocks.at[pl.ds(group(g) * RG, RG)], dst.at[pl.ds(g * RG, RG)], tok_s.at[i, g]
        )
        for i, (blocks, dst) in enumerate(((nm_all, nm_out), (og_all, og_out)))
        for g in range(G)
    ]
    parts(0)
    s_now = [0]

    def one_step(s, carry):
        s_now[0] = s
        x_send(s)
        spread_x()
        gather_x()
        chain_x()
        sum_x(s - H)
        finish_x(s - H * NZ)

        @pl.when(s == min(2, first - 1))
        def _():
            for kind in (og_kind, nm_kind):
                tok_second(kind, False)

        @pl.when(s == first - 1)
        def _():
            for kind in (og_kind, nm_kind):
                tok_last(kind, False)
            for copy in nm_outs:
                copy.start()

        @pl.when(s + 1 < Q)
        def _():
            parts(s + 1)

        start_z(s)
        spread_z()
        chain_z()
        exchange_z(s - H * (NZ - 1))
        finish_z(s - H * NZ)
        products(s - H * (NZ + 1 + far))

        @pl.when(s == first + pairs - 1 + 2 * H * NZ)
        def _():
            for i in range(RG):
                fin_send(group(0) * RG + i)

        return carry

    lax.fori_loop(0, Q + 2 * H * NZ, one_step, 0)

    for k in range(1, RG):
        fin_send(mine * RG + lax.rem(row + k, RG))
    for copy in nm_outs:
        copy.wait()
    for k in range(1, R):
        fin_copy(rpeer(k), rpeer(k)).wait_recv()
    down = acc_d[mine, fin_rows(row)]
    ngrad = acc_n[mine, fin_rows(row)]
    for k in range(1, R):
        down = down + fin_r[rpeer(k), 0].astype(F32)
        ngrad = ngrad + fin_r[rpeer(k), 1].astype(F32)
    x = x_ref[...].astype(F32)
    dt_mine[...] = to_lanes(jnp.sum(ngrad * gain * x, axis=1, keepdims=True))
    gn_mine[...] = jnp.sum(ngrad * x * scale, axis=0, keepdims=True)

    def dt_copy(src, dev):
        return remote(dt_mine, dt_all.at[src], dt_s.at[dev], dt_r.at[src], (row, dev))

    def gn_copy(src, dev):
        return remote(gn_mine, gn_all.at[src], gn_s.at[dev], gn_r.at[src], (dev, col))

    for k in range(1, C):
        dt_copy(col, cpeer(k)).start()
    for k in range(1, R):
        gn_copy(row, rpeer(k)).start()
    dt_all[col] = dt_mine[...]
    gn_all[row] = gn_mine[...]
    out_ref[...] = (x + down).astype(BF16)
    for dev in same_core:
        for kind in (og_kind, nm_kind):
            tok_copy(kind, row, dev).wait_send()
            tok_pass(kind, dev).wait_send()
    for kind in (og_kind, nm_kind):
        tok_copy(kind, row, other_core).wait_send()
    for k in range(1, R):
        fin_copy(row, rpeer(k)).wait_send()
    for k in range(1, C):
        sq_copy(col, cpeer(k)).wait_send()
    for q in range(Q - DS, Q):
        drain(q)
    for k in range(1, C):
        dt_copy(cpeer(k), cpeer(k)).wait_recv()
    dots = dt_all[0]
    for c in range(1, C):
        dots = dots + dt_all[c]
    dots = to_column(dots)
    ig_ref[...] = (
        og_ref[...].astype(F32)
        + scale * gain * ngrad
        - x * scale * scale * scale * dots / total_width
    ).astype(BF16)
    for k in range(1, R):
        gn_copy(rpeer(k), rpeer(k)).wait_recv()
    gain_sum = gn_all[0]
    for r in range(1, R):
        gain_sum = gain_sum + gn_all[r]
    gg_out[...] = gain_sum
    for k in range(1, R):
        gn_copy(row, rpeer(k)).wait_send()
    for k in range(1, C):
        dt_copy(col, cpeer(k)).wait_send()


def wgrad_kernel(nm_ref, og_ref, agx_ref, agz_ref, mg_ref, mu_ref, md_ref,
                 lo_ref, ig_ref, gn_ref, gw_ref, uw_ref, dw_ref, lo_out, ig_out, gn_out):
    p = pl.program_id(0)

    @pl.when(p == 0)
    def _():
        lo_out[...] = lo_ref[...]
        ig_out[...] = ig_ref[...]
        gn_out[...] = gn_ref[...]

    step = agx_ref.shape[1]
    feats = nm_ref.shape[1]
    per = step * 2 * W // BLK

    def tokens(i):
        return jnp.concatenate(
            [
                jnp.concatenate([ref[g, k, i] for k in range(step) for ref in (agx_ref, agz_ref)], axis=1)
                for g in range(G)
            ],
            axis=0,
        )

    for i, mask, dst in ((1, mg_ref, gw_ref), (2, mu_ref, uw_ref)):
        w = dot_tn(nm_ref[...], tokens(i))
        for r in range(feats // BLK):
            for b in range(per):
                at = (slice(r * BLK, (r + 1) * BLK), slice(b * BLK, (b + 1) * BLK))
                dst[at] = (w[at] * mask[r, p * per + b].astype(F32)).astype(BF16)
    w = dot_tn(tokens(0), og_ref[...])
    for r in range(feats // BLK):
        for b in range(per):
            at = (slice(b * BLK, (b + 1) * BLK), slice(r * BLK, (r + 1) * BLK))
            dw_ref[at] = (w[at] * md_ref[r, p * per + b].astype(F32)).astype(BF16)


def shards(R, C, layer_input, norm_gain, w_gate, w_up, w_down,
           mask_gate, mask_up, mask_down, out_grad):
    rows, feats = layer_input.shape
    hidden = w_gate.shape[1]
    tokens = rows * R
    NX = 1
    while (2 * NX) * (2 * NX) <= C:
        NX *= 2
    NZ = C // NX
    pairs = hidden // (2 * W)
    Q = G * pairs
    D = ring(Q, NZ)
    TG = tokens // G
    T = TG // (2 * NX)
    mask_down = mask_down.T
    vm = pl.BlockSpec(memory_space=pltpu.VMEM)
    sm = pl.BlockSpec(memory_space=pltpu.SMEM)
    hbm = pl.BlockSpec(memory_space=pl.ANY)
    dma = pltpu.SemaphoreType.DMA
    V = pltpu.VMEM
    out_shapes = (
        ((rows, feats), BF16), ((rows, feats), BF16), ((1, feats), F32),
        ((G, pairs, 3, TG, W), BF16), ((G, pairs, 3, TG, W), BF16),
        ((R, rows, feats), BF16), ((R, rows, feats), BF16),
    )
    scratch = [
        V((feats, hidden), BF16), V((feats, hidden), BF16), V((hidden, feats), BF16),
        V((R, rows, feats), BF16), V((R, rows, feats), BF16),
        V((1, LANES), F32), V((C, 1, LANES), F32),
        V((Q, NX, 2, 3, T, W), BF16), V((Q, NX, 2, 3, T, W), BF16), V((Q, 2, 3, T, W), BF16),
        V((Q, 2, 3, NX * T, W), BF16), V((Q, 2, 3, NX * T, W), BF16),
        V((Q, NX, 3, NX * T, W), BF16),
        V((Q, 3, TG, W), BF16), V((Q, 3, TG, W), BF16),
        V((G, TG, feats), F32), V((G, TG, feats), F32),
        V((R, 2, rows, feats), BF16), V((R, 2, rows, feats), BF16),
        V((1, feats), F32), V((R, 1, feats), F32),
        V((1, LANES), F32), V((C, 1, LANES), F32),
        dma((3,)),
        dma((R,)), dma((R,)), dma((R,)), dma((R,)), dma((R,)), dma((R,)),
        dma((C,)), dma((C,)),
        dma((DS, NX)), dma((D, NX)), dma((DS, 2)), dma((D, 2)), dma((DS, 2)), dma((D, 2)),
        dma((DS, NX)), dma((D, NX)), dma((DS, 2)), dma((D, 2)),
        dma((DS, 2, NX)), dma((D, 2, NX)), dma((DS, 2)), dma((D, 2)),
        dma((R,)), dma((R,)), dma((R,)), dma((R,)), dma((C,)), dma((C,)),
        dma((DS, 2)), dma((2, G)),
    ]
    layer_out, input_grad, gain_grad, agx, agz, nm, og = pl.pallas_call(
        functools.partial(layer_kernel, R, NZ, NX, float(feats * C)),
        out_shape=tuple(jax.ShapeDtypeStruct(s, t) for s, t in out_shapes),
        in_specs=[vm] * 3 + [sm] * 3 + [hbm] * 3,
        out_specs=tuple([vm] * 3 + [hbm] * 4),
        scratch_shapes=scratch,
        compiler_params=pltpu.CompilerParams(
            collective_id=0, has_side_effects=True, vmem_limit_bytes=67043328
        ),
    )(layer_input, norm_gain[None, :], out_grad, mask_gate, mask_up, mask_down,
      w_gate, w_up, w_down)

    whole = lambda p: (0, 0)
    step = 2 if pairs % 2 == 0 else 1
    gate_wgrad, up_wgrad, down_wgrad, layer_out, input_grad, gain_grad = pl.pallas_call(
        wgrad_kernel,
        grid=(pairs // step,),
        out_shape=(
            jax.ShapeDtypeStruct((feats, hidden), BF16),
            jax.ShapeDtypeStruct((feats, hidden), BF16),
            jax.ShapeDtypeStruct((hidden, feats), BF16),
            jax.ShapeDtypeStruct((rows, feats), BF16),
            jax.ShapeDtypeStruct((rows, feats), BF16),
            jax.ShapeDtypeStruct((1, feats), F32),
        ),
        in_specs=[
            pl.BlockSpec((tokens, feats), whole),
            pl.BlockSpec((tokens, feats), whole),
            pl.BlockSpec((G, step, 3, TG, W), lambda p: (0, p, 0, 0, 0)),
            pl.BlockSpec((G, step, 3, TG, W), lambda p: (0, p, 0, 0, 0)),
            sm, sm, sm,
            pl.BlockSpec((rows, feats), whole),
            pl.BlockSpec((rows, feats), whole),
            pl.BlockSpec((1, feats), whole),
        ],
        out_specs=(
            pl.BlockSpec((feats, step * 2 * W), lambda p: (0, p)),
            pl.BlockSpec((feats, step * 2 * W), lambda p: (0, p)),
            pl.BlockSpec((step * 2 * W, feats), lambda p: (p, 0)),
            pl.BlockSpec((rows, feats), whole),
            pl.BlockSpec((rows, feats), whole),
            pl.BlockSpec((1, feats), whole),
        ),
        compiler_params=pltpu.CompilerParams(vmem_limit_bytes=67043328),
    )(nm.reshape(tokens, feats), og.reshape(tokens, feats),
      agx, agz,
      mask_gate, mask_up, mask_down, layer_out, input_grad, gain_grad)
    return (layer_out, input_grad, gain_grad[0], gate_wgrad, up_wgrad, down_wgrad)


def solution(mesh):
    placed = (
        P("row", "col"),
        P("col"),
        P("col", "row"),
        P("col", "row"),
        P("row", "col"),
        P("col", "row"),
        P("col", "row"),
        P("row", "col"),
        P("row", "col"),
    )
    return jax.shard_map(
        functools.partial(shards, mesh.shape["row"], mesh.shape["col"]),
        mesh=mesh,
        in_specs=placed,
        out_specs=(
            P("row", "col"),
            P("row", "col"),
            P("col"),
            P("col", "row"),
            P("col", "row"),
            P("row", "col"),
        ),
        check_vma=False,
    )
```

```python
import functools

import jax
import jax.numpy as jnp
from jax import lax
from jax.experimental import pallas as pl
from jax.experimental.pallas import tpu as pltpu
from jax.sharding import PartitionSpec as P

BLK = 128
LANES = 128
MESH = pl.DeviceIdType.MESH
F32 = jnp.float32
BF16 = jnp.bfloat16
norm_eps = 1e-05


def dot_nn(left, right):
    return lax.dot_general(left, right, (((1,), (0,)), ((), ())), preferred_element_type=F32)


def dot_nt(left, right):
    return lax.dot_general(left, right, (((1,), (1,)), ((), ())), preferred_element_type=F32)


def dot_tn(left, right):
    return lax.dot_general(left, right, (((0,), (0,)), ((), ())), preferred_element_type=F32)


G = 2
W = 128
H = 2


DS = 3


def ring(Q, NZ):
    return min(Q, H * NZ + 2)


def layer_kernel(
    R, NZ, NX, total_width,
    x_ref, gain_ref, og_ref, mg_ref, mu_ref, md_ref, wg_hbm, wu_hbm, wd_hbm,
    out_ref, ig_ref, gg_out, agx_out, agz_out, nm_out, og_out,
    wg, wu, wd, nm_all, og_all, x_other, sq_mine, sq_all,
    xp, xr, xc, zp, zc, zx, agx, agz,
    acc_d, acc_n, fin_s, fin_r, gn_mine, gn_all, dt_mine, dt_other, dt_all,
    w_sem, og_s, og_f, og_r, nm_s, nm_f, nm_r, xo_s, xo_r, sq_s, sq_r,
    x_s, x_r, xc_s, xc_r, zc_s, zc_r, zx_s, zx_r, axz_s, axz_r, axx_s, axx_r, az_s, az_r,
    fin_ss, fin_rs, gn_s, gn_r, dt_s, dt_r, out_s, tok_s,
):
    C = NZ * NX
    row = lax.axis_index("row")
    col = lax.axis_index("col")
    mz = col // NX
    mx = lax.rem(col, NX)
    rows, feats = x_ref.shape
    hidden = wg.shape[1]
    pairs = hidden // (2 * W)
    Q = G * pairs
    D = ring(Q, NZ)
    RG = R // G
    TG = RG * rows
    T = TG // (2 * NX)
    mine = row // RG
    low = mz == 0
    high = mz == NZ - 1
    end = jnp.logical_or(low, high)
    half = mz // (NZ - 1)
    far = jnp.maximum(mz, NZ - 1 - mz)

    def rpeer(k):
        return lax.rem(row + k, R)

    def cpeer(k):
        return lax.rem(col + k, C)

    def xpeer(k):
        return lax.rem(mx + k, NX)

    first = (pairs + 1) // 2

    def place(q):
        return jnp.where(jnp.logical_or(q < first, q >= first + pairs), 1, 0)

    def pair(q):
        return jnp.where(q < first, q, jnp.where(q < first + pairs, q - first, q - pairs))

    def fresh(q):
        return jnp.logical_or(q < first, jnp.logical_and(q >= 2 * first, q < first + pairs))

    def group(place):
        return lax.rem(mine + 1 + place, G)

    other_core = row + 1 - 2 * lax.rem(row, 2)
    same_core = [lax.rem(row + 2 * k, R) for k in range(1, R // 2)]

    def remote(src, dst, ssem, rsem, dev):
        return pltpu.make_async_remote_copy(
            src_ref=src, dst_ref=dst, send_sem=ssem, recv_sem=rsem,
            device_id=dev, device_id_type=MESH,
        )

    def both(*conds):
        return functools.reduce(jnp.logical_and, conds)

    def at_s(q):
        return lax.rem(q, DS)

    def at_r(q):
        return lax.rem(q, D)

    def send(make, q):
        @pl.when(q >= DS)
        def _():
            make(q - DS).wait_send()

        make(q).start()

    def live(q):
        return jnp.logical_and(q >= 0, q < Q)

    barrier = pltpu.get_barrier_semaphore()
    for k in range(1, R):
        pl.semaphore_signal(barrier, inc=1, device_id=(rpeer(k), col), device_id_type=MESH)
    for k in range(1, C):
        for r in (row, other_core):
            pl.semaphore_signal(barrier, inc=1, device_id=(r, cpeer(k)), device_id_type=MESH)
    cuts = sorted({0, min(1, pairs), min(2, pairs), pairs})
    early = min(2, first)

    def loads(i):
        cols = pl.ds(cuts[i] * 2 * W, (cuts[i + 1] - cuts[i]) * 2 * W)
        return (
            pltpu.make_async_copy(wd_hbm.at[cols], wd.at[cols], w_sem.at[0, i]),
            pltpu.make_async_copy(wg_hbm.at[:, cols], wg.at[:, cols], w_sem.at[1, i]),
            pltpu.make_async_copy(wu_hbm.at[:, cols], wu.at[:, cols], w_sem.at[2, i]),
        )

    for i in range(len(cuts) - 1):
        for load in loads(i):
            load.start()
    def keep(mask_ref, r, c):
        return jnp.full((BLK, BLK), mask_ref[r, c].astype(F32), F32).astype(BF16)

    def columns(p):
        return pl.ds(pl.multiple_of(p * (2 * W), 2 * W), 2 * W)

    def mask_pair(p):
        for i, cut in enumerate(cuts[:-1]):

            @pl.when(p == cut)
            def _():
                for load in loads(i):
                    load.wait()

        per = 2 * W // BLK
        for b in range(per):
            at = pl.ds(pl.multiple_of(p * (2 * W) + b * BLK, BLK), BLK)
            block = p * per + b
            for r in range(feats // BLK):
                f = slice(r * BLK, (r + 1) * BLK)
                wd[at, f] = wd[at, f] * keep(md_ref, r, block)
                wg[f, at] = wg[f, at] * keep(mg_ref, r, block)
                wu[f, at] = wu[f, at] * keep(mu_ref, r, block)

    og_all[row] = og_ref[...]
    x = x_ref[...].astype(F32)
    tok = lax.broadcasted_iota(jnp.int32, (rows, LANES), 0)
    lane = lax.broadcasted_iota(jnp.int32, (rows, LANES), 1)
    diag = tok == lane

    def to_lanes(column):
        return jnp.sum(jnp.where(diag, column, 0.0), axis=0, keepdims=True)

    def to_column(line):
        return jnp.sum(jnp.where(diag, line, 0.0), axis=1, keepdims=True)

    sq_mine[...] = to_lanes(jnp.sum(x * x, axis=1, keepdims=True))
    sq_all[0, col] = sq_mine[...]
    pl.semaphore_wait(barrier, R - 1 + 2 * (C - 1))

    def by_core(w):
        return (row, other_core)[w], range(1 - w, C)

    def sq_copy(w, src, dev):
        r, _ = by_core(w)
        return remote(sq_mine, sq_all.at[w, src], sq_s.at[w, dev], sq_r.at[w, src], (r, dev))

    x_copy_other = remote(x_ref, x_other, xo_s.at[0], xo_r.at[0], (other_core, col))
    for w in range(2):
        for k in by_core(w)[1]:
            sq_copy(w, col, cpeer(k)).start()
    x_copy_other.start()

    def tok_copy(kind, src, dev):
        blocks, ssem, _, rsem = kind
        return remote(blocks.at[src], blocks.at[src], ssem.at[dev], rsem.at[src], (dev, col))

    def tok_pass(kind, src):
        blocks, _, fsem, rsem = kind
        return remote(blocks.at[src], blocks.at[src], fsem.at[src], rsem.at[src], (other_core, col))

    og_kind = (og_all, og_s, og_f, og_r)
    nm_kind = (nm_all, nm_s, nm_f, nm_r)

    def tok_first(kind):
        for dev in same_core:
            tok_copy(kind, row, dev).start()

    def tok_second(kind, own):
        for src in same_core:

            @pl.when((src // RG == mine) == own)
            def _():
                tok_copy(kind, src, src).wait_recv()
                tok_pass(kind, src).start()

    def tok_last(kind, own):
        for k in range(1, R):
            src = rpeer(k)
            missing = jnp.logical_and(lax.rem(src, 2) != lax.rem(row, 2), (src // RG == mine) == own)
            if kind is nm_kind:
                missing = jnp.logical_and(missing, src != other_core)

            @pl.when(missing)
            def _():
                tok_copy(kind, src, src).wait_recv()

    tok_copy(og_kind, row, other_core).start()
    tok_first(og_kind)
    for p in range(early):
        mask_pair(jnp.int32(p))
    acc_d[...] = jnp.zeros_like(acc_d)
    acc_n[...] = jnp.zeros_like(acc_n)
    gain = gain_ref[...]

    def row_scale(w):
        for k in by_core(w)[1]:
            sq_copy(w, cpeer(k), cpeer(k)).wait_recv()
        total = sq_all[w, 0]
        for c in range(1, C):
            total = total + sq_all[w, c]
        return lax.rsqrt(to_column(total) / total_width + norm_eps)

    scale = row_scale(0)
    nm_all[row] = (x * scale * gain).astype(BF16)
    tok_first(nm_kind)
    x_copy_other.wait_recv()
    scale_other = row_scale(1)
    nm_all[other_core] = (x_other[...].astype(F32) * scale_other * gain).astype(BF16)

    def parts(q):
        p = pair(q)
        grp = group(place(q))
        cols = columns(p)

        @pl.when(jnp.logical_and(fresh(q), q >= early))
        def _():
            mask_pair(p)

        ogt = og_all[pl.ds(grp * RG, RG)].reshape(TG, feats)
        nmt = nm_all[pl.ds(grp * RG, RG)].reshape(TG, feats)
        for i in range(3):
            if i == 0:
                v = dot_nt(ogt, wd[cols, :])
            else:
                v = dot_nn(nmt, (wg, wu)[i - 1][:, cols])
            v = v.astype(BF16)
            for xx in range(NX):
                for h in range(2):
                    b = xx * 2 + h
                    xp[q, xx, h, i] = v[b * T : (b + 1) * T, :W]
            for h in range(2):
                zp[q, h, i] = v[h * NX * T : (h + 1) * NX * T, W:]

    def znb(step):
        return (row, (mz + step) * NX + mx)

    def along_x(k, out):
        dev = xpeer(k)
        return (mx, dev, k - 1) if out else (dev, dev, NX - k - 1)

    def x_copy(q, k, out):
        src, dev, i = along_x(k, out)
        return remote(
            xp.at[q, dev], xr.at[q, src], x_s.at[at_s(q), i], x_r.at[at_r(q), i],
            (row, mz * NX + dev),
        )

    def xc_copy(q, h, step):
        return remote(
            xp.at[q, mx, h], xc.at[q, h], xc_s.at[at_s(q), h], xc_r.at[at_r(q), h], znb(step)
        )

    def zc_copy(q, h, step):
        return remote(
            zp.at[q, h], zc.at[q, h], zc_s.at[at_s(q), h], zc_r.at[at_r(q), h], znb(step)
        )

    def zx_copy(q, k, out):
        src, dev, i = along_x(k, out)
        return remote(
            zp.at[q, half], zx.at[q, src], zx_s.at[at_s(q), i], zx_r.at[at_r(q), i],
            (row, mz * NX + dev),
        )

    def x_tokens(src, h):
        return pl.ds(pl.multiple_of((src * 2 + h) * T, T), T)

    def z_tokens(h):
        return pl.ds(pl.multiple_of(h * (NX * T), NX * T), NX * T)

    def axz_copy(q, h, step):
        block = agx.at[q, :, x_tokens(mx, h)]
        return remote(block, block, axz_s.at[at_s(q), h], axz_r.at[at_r(q), h], znb(step))

    def axx_copy(q, h, k, out):
        src, dev, i = along_x(k, out)
        block = agx.at[q, :, x_tokens(src, h)]
        return remote(
            block, block, axx_s.at[at_s(q), h, i], axx_r.at[at_r(q), h, i],
            (row, mz * NX + dev),
        )

    def az_copy(q, h, step):
        block = agz.at[q, :, z_tokens(h)]
        return remote(block, block, az_s.at[at_s(q), h], az_r.at[at_r(q), h], znb(step))

    def pointwise(gate, up, da):
        sig = jax.nn.sigmoid(gate)
        return (
            (gate * sig * up).astype(BF16),
            (da * up * sig * (1.0 + gate * (1.0 - sig))).astype(BF16),
            (da * gate * sig).astype(BF16),
        )

    def x_send(q):
        @pl.when(live(q))
        def _():
            for k in range(1, NX):
                send(lambda q: x_copy(q, k, True), q)

    def share_x(q, h):
        for k in range(1, NX):
            send(lambda q: axx_copy(q, h, k, True), q)

    def spread_x():
        for h, step, hops in ((0, 1, mz), (1, -1, NZ - 1 - mz)):
            q = s_now[0] - H * (NZ + hops)

            @pl.when(both(live(q), hops > 0))
            def _():
                axz_copy(q, h, -step).wait_recv()

                @pl.when(hops < NZ - 1)
                def _():
                    send(lambda q: axz_copy(q, h, step), q)

                share_x(q, h)

    def spread_z():
        for h, step, hops in ((0, 1, mz), (1, -1, NZ - 1 - mz)):
            q = s_now[0] - H * (NZ + hops)

            @pl.when(both(live(q), hops > 0))
            def _():
                az_copy(q, h, -step).wait_recv()

                @pl.when(hops < NZ - 1)
                def _():
                    send(lambda q: az_copy(q, h, step), q)

    def chain_x():
        for h, step, hops in ((1, 1, mz), (0, -1, NZ - 1 - mz)):
            q = s_now[0] - H * (1 + hops)

            @pl.when(both(live(q), hops > 0, hops < NZ - 1))
            def _():
                xc_copy(q, h, -step).wait_recv()
                xp[q, mx, h] = (xp[q, mx, h].astype(F32) + xc[q, h].astype(F32)).astype(BF16)
                send(lambda q: xc_copy(q, h, step), q)

    def chain_z():
        for h, step, hops in ((1, 1, mz), (0, -1, NZ - 1 - mz)):
            q = s_now[0] - H * hops

            @pl.when(both(live(q), hops > 0, hops < NZ - 1))
            def _():
                zc_copy(q, h, -step).wait_recv()
                zp[q, h] = (zp[q, h].astype(F32) + zc[q, h].astype(F32)).astype(BF16)
                send(lambda q: zc_copy(q, h, step), q)

    def sum_x(q):
        @pl.when(live(q))
        def _():
            for k in range(1, NX):
                x_copy(q, k, False).wait_recv()
            for h in range(2):
                v = xp[q, mx, h].astype(F32)
                for k in range(1, NX):
                    v = v + xr[q, xpeer(k), h].astype(F32)
                xp[q, mx, h] = v.astype(BF16)

            @pl.when(low)
            def _():
                send(lambda q: xc_copy(q, 1, 1), q)

            @pl.when(high)
            def _():
                send(lambda q: xc_copy(q, 0, -1), q)

    def finish_x(q):
        for h, at_end, step in ((0, low, 1), (1, high, -1)):

            @pl.when(both(live(q), at_end))
            def _():
                xc_copy(q, h, step).wait_recv()
                da, gate, up = (
                    xp[q, mx, h, i].astype(F32) + xc[q, h, i].astype(F32) for i in range(3)
                )
                for i, v in enumerate(pointwise(gate, up, da)):
                    agx[q, i, x_tokens(mx, h)] = v
                send(lambda q: axz_copy(q, h, step), q)
                share_x(q, h)

    def start_z(q):
        @pl.when(both(live(q), low))
        def _():
            send(lambda q: zc_copy(q, 1, 1), q)

        @pl.when(both(live(q), high))
        def _():
            send(lambda q: zc_copy(q, 0, -1), q)

    def exchange_z(q):
        for h, at_end, step in ((0, low, 1), (1, high, -1)):

            @pl.when(both(live(q), at_end))
            def _():
                zc_copy(q, h, step).wait_recv()
                zp[q, h] = (zp[q, h].astype(F32) + zc[q, h].astype(F32)).astype(BF16)
                for k in range(1, NX):
                    send(lambda q: zx_copy(q, k, True), q)

    def finish_z(q):
        for h, at_end, step in ((0, low, 1), (1, high, -1)):

            @pl.when(both(live(q), at_end))
            def _():
                for k in range(1, NX):
                    zx_copy(q, k, False).wait_recv()

                def summed(i):
                    v = zp[q, h, i].astype(F32)
                    for k in range(1, NX):
                        v = v + zx[q, xpeer(k), i].astype(F32)
                    return v

                da, gate, up = (summed(i) for i in range(3))
                for i, v in enumerate(pointwise(gate, up, da)):
                    agz[q, i, h * NX * T : (h + 1) * NX * T] = v
                send(lambda q: az_copy(q, h, step), q)

    def gather_x():
        for h, hops in ((0, mz), (1, NZ - 1 - mz)):
            q = s_now[0] - H * (NZ + 1 + hops)

            @pl.when(live(q))
            def _():
                for k in range(1, NX):
                    axx_copy(q, h, k, False).wait_recv()

    def out_copies(q):
        return (
            pltpu.make_async_copy(agx.at[q], agx_out.at[place(q), pair(q)], out_s.at[at_s(q), 0]),
            pltpu.make_async_copy(agz.at[q], agz_out.at[place(q), pair(q)], out_s.at[at_s(q), 1]),
        )

    def products(q):
        @pl.when(live(q))
        def _():
            @pl.when(q >= DS)
            def _():
                for copy in out_copies(q - DS):
                    copy.wait()

            for copy in out_copies(q):
                copy.start()
            grp = group(place(q))
            cols = columns(pair(q))

            def tokens(i):
                return jnp.concatenate([agx[q, i], agz[q, i]], axis=1)

            acc_d[grp] += dot_nn(tokens(0), wd[cols, :])
            acc_n[grp] += dot_nt(tokens(1), wg[:, cols]) + dot_nt(tokens(2), wu[:, cols])

    def drain(q):
        for k in range(1, NX):
            x_copy(q, k, True).wait_send()
            for h in range(2):
                axx_copy(q, h, k, True).wait_send()
        for h, step, hops in ((1, 1, mz), (0, -1, NZ - 1 - mz)):

            @pl.when(hops < NZ - 1)
            def _():
                xc_copy(q, h, step).wait_send()
                zc_copy(q, h, step).wait_send()
                axz_copy(q, 1 - h, step).wait_send()
                az_copy(q, 1 - h, step).wait_send()

        @pl.when(end)
        def _():
            for k in range(1, NX):
                zx_copy(q, k, True).wait_send()

        for copy in out_copies(q):
            copy.wait()

    def fin_copy(src, dev):
        return remote(
            fin_s.at[dev], fin_r.at[src], fin_ss.at[dev], fin_rs.at[src], (dev, col)
        )

    def fin_rows(r):
        return pl.ds(pl.multiple_of(lax.rem(r, RG) * rows, rows), rows)

    def fin_send(r):
        fin_s[r, 0] = acc_d[r // RG, fin_rows(r)].astype(BF16)
        fin_s[r, 1] = acc_n[r // RG, fin_rows(r)].astype(BF16)
        fin_copy(row, r).start()

    for kind in (og_kind, nm_kind):
        tok_second(kind, True)
    for kind in (og_kind, nm_kind):
        tok_last(kind, True)
    nm_outs = [
        pltpu.make_async_copy(
            blocks.at[pl.ds(group(g) * RG, RG)], dst.at[pl.ds(g * RG, RG)], tok_s.at[i, g]
        )
        for i, (blocks, dst) in enumerate(((nm_all, nm_out), (og_all, og_out)))
        for g in range(G)
    ]
    parts(0)
    s_now = [0]

    def one_step(s, carry):
        s_now[0] = s
        x_send(s)
        start_z(s)
        spread_x()
        gather_x()
        chain_x()
        sum_x(s - H)
        finish_x(s - H * NZ)

        @pl.when(s == min(2, first - 1))
        def _():
            for kind in (og_kind, nm_kind):
                tok_second(kind, False)

        @pl.when(s == first - 1)
        def _():
            for kind in (og_kind, nm_kind):
                tok_last(kind, False)
            for copy in nm_outs:
                copy.start()

        @pl.when(s + 1 < Q)
        def _():
            parts(s + 1)

        spread_z()
        chain_z()
        exchange_z(s - H * (NZ - 1))
        finish_z(s - H * NZ)
        products(s - H * (NZ + 1 + far))

        @pl.when(s == first + pairs - 1 + 2 * H * NZ)
        def _():
            for i in range(RG):
                fin_send(group(0) * RG + i)

        return carry

    lax.fori_loop(0, Q + 2 * H * NZ, one_step, 0)

    for k in range(1, RG):
        fin_send(mine * RG + lax.rem(row + k, RG))
    for copy in nm_outs:
        copy.wait()
    x_peer = x_other[...].astype(F32)
    part = acc_n[mine, fin_rows(other_core)]
    dt_other[...] = to_lanes(jnp.sum(part * gain * x_peer, axis=1, keepdims=True))

    def dt_copy(w, src, dev):
        r, _ = by_core(w)
        return remote(
            (dt_mine, dt_other)[w], dt_all.at[w, src], dt_s.at[w, dev], dt_r.at[w, src], (r, dev)
        )

    def gn_copy(src, dev):
        return remote(gn_mine, gn_all.at[src], gn_s.at[dev], gn_r.at[src], (dev, col))

    for k in by_core(1)[1]:
        dt_copy(1, col, cpeer(k)).start()
    down = acc_d[mine, fin_rows(row)]
    ngrad = acc_n[mine, fin_rows(row)]
    for k in range(1, R):
        src = rpeer(k)

        @pl.when(src != other_core)
        def _():
            fin_copy(src, src).wait_recv()

    def others(i):
        total = jnp.zeros((rows, feats), F32)
        for k in range(1, R // 2):
            for core in range(2):
                total = total + fin_r[lax.rem(row // 2 + k, R // 2) * 2 + core, i].astype(F32)
        return total

    down = down + others(0)
    ngrad = ngrad + others(1)
    x = x_ref[...].astype(F32)
    dt_mine[...] = to_lanes(jnp.sum(ngrad * gain * x, axis=1, keepdims=True))
    gn_mine[...] = jnp.sum(ngrad * x * scale + part * x_peer * scale_other, axis=0, keepdims=True)
    for k in by_core(0)[1]:
        dt_copy(0, col, cpeer(k)).start()
    for k in range(1, R):
        gn_copy(row, rpeer(k)).start()
    dt_all[0, col] = dt_mine[...]
    gn_all[row] = gn_mine[...]
    fin_copy(other_core, other_core).wait_recv()
    down = down + fin_r[other_core, 0].astype(F32)
    ngrad = ngrad + fin_r[other_core, 1].astype(F32)
    out_ref[...] = (x + down).astype(BF16)
    for dev in same_core:
        for kind in (og_kind, nm_kind):
            tok_copy(kind, row, dev).wait_send()
            tok_pass(kind, dev).wait_send()
    tok_copy(og_kind, row, other_core).wait_send()
    x_copy_other.wait_send()
    for k in range(1, R):
        fin_copy(row, rpeer(k)).wait_send()
    for w in range(2):
        for k in by_core(w)[1]:
            sq_copy(w, col, cpeer(k)).wait_send()
    for q in range(Q - DS, Q):
        drain(q)
    for w in range(2):
        for k in by_core(w)[1]:
            dt_copy(w, cpeer(k), cpeer(k)).wait_recv()
    dots = dt_all[0, 0] + dt_all[1, 0]
    for c in range(1, C):
        dots = dots + dt_all[0, c] + dt_all[1, c]
    dots = to_column(dots)
    ig_ref[...] = (
        og_ref[...].astype(F32)
        + scale * gain * ngrad
        - x * scale * scale * scale * dots / total_width
    ).astype(BF16)
    for k in range(1, R):
        gn_copy(rpeer(k), rpeer(k)).wait_recv()
    gain_sum = gn_all[0]
    for r in range(1, R):
        gain_sum = gain_sum + gn_all[r]
    gg_out[...] = gain_sum
    for k in range(1, R):
        gn_copy(row, rpeer(k)).wait_send()
    for w in range(2):
        for k in by_core(w)[1]:
            dt_copy(w, col, cpeer(k)).wait_send()


def wgrad_kernel(nm_ref, og_ref, agx_ref, agz_ref, mg_ref, mu_ref, md_ref,
                 lo_ref, ig_ref, gn_ref, gw_ref, uw_ref, dw_ref, lo_out, ig_out, gn_out):
    p = pl.program_id(0)

    @pl.when(p == 0)
    def _():
        lo_out[...] = lo_ref[...]
        ig_out[...] = ig_ref[...]
        gn_out[...] = gn_ref[...]

    step = agx_ref.shape[1]
    feats = nm_ref.shape[1]
    per = step * 2 * W // BLK

    def tokens(i):
        return jnp.concatenate(
            [
                jnp.concatenate([ref[g, k, i] for k in range(step) for ref in (agx_ref, agz_ref)], axis=1)
                for g in range(G)
            ],
            axis=0,
        )

    for i, mask, dst in ((1, mg_ref, gw_ref), (2, mu_ref, uw_ref)):
        w = dot_tn(nm_ref[...], tokens(i))
        for r in range(feats // BLK):
            for b in range(per):
                at = (slice(r * BLK, (r + 1) * BLK), slice(b * BLK, (b + 1) * BLK))
                dst[at] = (w[at] * mask[r, p * per + b].astype(F32)).astype(BF16)
    w = dot_tn(tokens(0), og_ref[...])
    for r in range(feats // BLK):
        for b in range(per):
            at = (slice(b * BLK, (b + 1) * BLK), slice(r * BLK, (r + 1) * BLK))
            dw_ref[at] = (w[at] * md_ref[r, p * per + b].astype(F32)).astype(BF16)


def shards(R, C, layer_input, norm_gain, w_gate, w_up, w_down,
           mask_gate, mask_up, mask_down, out_grad):
    rows, feats = layer_input.shape
    hidden = w_gate.shape[1]
    tokens = rows * R
    NX = 1
    while (2 * NX) * (2 * NX) <= C:
        NX *= 2
    NZ = C // NX
    pairs = hidden // (2 * W)
    Q = G * pairs
    D = ring(Q, NZ)
    TG = tokens // G
    T = TG // (2 * NX)
    mask_down = mask_down.T
    vm = pl.BlockSpec(memory_space=pltpu.VMEM)
    sm = pl.BlockSpec(memory_space=pltpu.SMEM)
    hbm = pl.BlockSpec(memory_space=pl.ANY)
    dma = pltpu.SemaphoreType.DMA
    V = pltpu.VMEM
    out_shapes = (
        ((rows, feats), BF16), ((rows, feats), BF16), ((1, feats), F32),
        ((G, pairs, 3, TG, W), BF16), ((G, pairs, 3, TG, W), BF16),
        ((R, rows, feats), BF16), ((R, rows, feats), BF16),
    )
    scratch = [
        V((feats, hidden), BF16), V((feats, hidden), BF16), V((hidden, feats), BF16),
        V((R, rows, feats), BF16), V((R, rows, feats), BF16),
        V((rows, feats), BF16), V((1, LANES), F32), V((2, C, 1, LANES), F32),
        V((Q, NX, 2, 3, T, W), BF16), V((Q, NX, 2, 3, T, W), BF16), V((Q, 2, 3, T, W), BF16),
        V((Q, 2, 3, NX * T, W), BF16), V((Q, 2, 3, NX * T, W), BF16),
        V((Q, NX, 3, NX * T, W), BF16),
        V((Q, 3, TG, W), BF16), V((Q, 3, TG, W), BF16),
        V((G, TG, feats), F32), V((G, TG, feats), F32),
        V((R, 2, rows, feats), BF16), V((R, 2, rows, feats), BF16),
        V((1, feats), F32), V((R, 1, feats), F32),
        V((1, LANES), F32), V((1, LANES), F32), V((2, C, 1, LANES), F32),
        dma((3, 3)),
        dma((R,)), dma((R,)), dma((R,)), dma((R,)), dma((R,)), dma((R,)),
        dma((1,)), dma((1,)), dma((2, C)), dma((2, C)),
        dma((DS, NX - 1)), dma((D, NX - 1)), dma((DS, 2)), dma((D, 2)), dma((DS, 2)), dma((D, 2)),
        dma((DS, NX - 1)), dma((D, NX - 1)), dma((DS, 2)), dma((D, 2)),
        dma((DS, 2, NX - 1)), dma((D, 2, NX - 1)), dma((DS, 2)), dma((D, 2)),
        dma((R,)), dma((R,)), dma((R,)), dma((R,)), dma((2, C)), dma((2, C)),
        dma((DS, 2)), dma((2, G)),
    ]
    layer_out, input_grad, gain_grad, agx, agz, nm, og = pl.pallas_call(
        functools.partial(layer_kernel, R, NZ, NX, float(feats * C)),
        out_shape=tuple(jax.ShapeDtypeStruct(s, t) for s, t in out_shapes),
        in_specs=[vm] * 3 + [sm] * 3 + [hbm] * 3,
        out_specs=tuple([vm] * 3 + [hbm] * 4),
        scratch_shapes=scratch,
        compiler_params=pltpu.CompilerParams(
            collective_id=0, has_side_effects=True, vmem_limit_bytes=67043328
        ),
    )(layer_input, norm_gain[None, :], out_grad, mask_gate, mask_up, mask_down,
      w_gate, w_up, w_down)

    whole = lambda p: (0, 0)
    step = 2 if pairs % 2 == 0 else 1
    gate_wgrad, up_wgrad, down_wgrad, layer_out, input_grad, gain_grad = pl.pallas_call(
        wgrad_kernel,
        grid=(pairs // step,),
        out_shape=(
            jax.ShapeDtypeStruct((feats, hidden), BF16),
            jax.ShapeDtypeStruct((feats, hidden), BF16),
            jax.ShapeDtypeStruct((hidden, feats), BF16),
            jax.ShapeDtypeStruct((rows, feats), BF16),
            jax.ShapeDtypeStruct((rows, feats), BF16),
            jax.ShapeDtypeStruct((1, feats), F32),
        ),
        in_specs=[
            pl.BlockSpec((tokens, feats), whole),
            pl.BlockSpec((tokens, feats), whole),
            pl.BlockSpec((G, step, 3, TG, W), lambda p: (0, p, 0, 0, 0)),
            pl.BlockSpec((G, step, 3, TG, W), lambda p: (0, p, 0, 0, 0)),
            sm, sm, sm,
            pl.BlockSpec((rows, feats), whole),
            pl.BlockSpec((rows, feats), whole),
            pl.BlockSpec((1, feats), whole),
        ],
        out_specs=(
            pl.BlockSpec((feats, step * 2 * W), lambda p: (0, p)),
            pl.BlockSpec((feats, step * 2 * W), lambda p: (0, p)),
            pl.BlockSpec((step * 2 * W, feats), lambda p: (p, 0)),
            pl.BlockSpec((rows, feats), whole),
            pl.BlockSpec((rows, feats), whole),
            pl.BlockSpec((1, feats), whole),
        ),
        compiler_params=pltpu.CompilerParams(vmem_limit_bytes=67043328),
    )(nm.reshape(tokens, feats), og.reshape(tokens, feats),
      agx, agz,
      mask_gate, mask_up, mask_down, layer_out, input_grad, gain_grad)
    return (layer_out, input_grad, gain_grad[0], gate_wgrad, up_wgrad, down_wgrad)


def solution(mesh):
    placed = (
        P("row", "col"),
        P("col"),
        P("col", "row"),
        P("col", "row"),
        P("row", "col"),
        P("col", "row"),
        P("col", "row"),
        P("row", "col"),
        P("row", "col"),
    )
    return jax.shard_map(
        functools.partial(shards, mesh.shape["row"], mesh.shape["col"]),
        mesh=mesh,
        in_specs=placed,
        out_specs=(
            P("row", "col"),
            P("row", "col"),
            P("col"),
            P("col", "row"),
            P("col", "row"),
            P("row", "col"),
        ),
        check_vma=False,
    )
```

```python
import functools

import jax
import jax.numpy as jnp
from jax import lax
from jax.experimental import pallas as pl
from jax.experimental.pallas import tpu as pltpu
from jax.sharding import PartitionSpec as P

BLK = 128
LANES = 128
MESH = pl.DeviceIdType.MESH
F32 = jnp.float32
BF16 = jnp.bfloat16
norm_eps = 1e-05


def dot_nn(left, right):
    return lax.dot_general(left, right, (((1,), (0,)), ((), ())), preferred_element_type=F32)


def dot_nt(left, right):
    return lax.dot_general(left, right, (((1,), (1,)), ((), ())), preferred_element_type=F32)


def dot_tn(left, right):
    return lax.dot_general(left, right, (((0,), (0,)), ((), ())), preferred_element_type=F32)


G = 2
W = 128
H = 2


DS = 2


def ring(Q, NZ):
    return min(Q, H * NZ)


def layer_kernel(
    R, NZ, NX, total_width,
    x_ref, gain_ref, og_ref, mg_ref, mu_ref, md_ref, wg_hbm, wu_hbm, wd_hbm,
    out_ref, ig_ref, gg_out, agx_out, agz_out, nm_out, og_out,
    wg, wu, wd, nm_all, og_all, x_other, sq_mine, sq_all,
    xp, xr, xc, zp, zc, zx, agx, agz,
    acc_d, acc_n, fin_s, fin_r, gn_mine, gn_all, dt_mine, dt_other, dt_all,
    w_sem, og_s, og_f, og_r, nm_s, nm_f, nm_r, xo_s, xo_r, sq_s, sq_r,
    x_s, x_r, xc_s, xc_r, zc_s, zc_r, zx_s, zx_r, axz_s, axz_r, axx_s, axx_r, az_s, az_r,
    fin_ss, fin_rs, gn_s, gn_r, dt_s, dt_r, out_s, tok_s,
):
    C = NZ * NX
    row = lax.axis_index("row")
    col = lax.axis_index("col")
    mz = col // NX
    mx = lax.rem(col, NX)
    rows, feats = x_ref.shape
    hidden = wg.shape[1]
    pairs = hidden // (2 * W)
    Q = G * pairs
    D = ring(Q, NZ)
    RG = R // G
    TG = RG * rows
    T = TG // (2 * NX)
    mine = row // RG
    low = mz == 0
    high = mz == NZ - 1
    end = jnp.logical_or(low, high)
    half = mz // (NZ - 1)
    far = jnp.maximum(mz, NZ - 1 - mz)

    def rpeer(k):
        return lax.rem(row + k, R)

    def cpeer(k):
        return lax.rem(col + k, C)

    def xpeer(k):
        return lax.rem(mx + k, NX)

    first = (pairs + 1) // 2

    def place(q):
        return jnp.where(jnp.logical_or(q < first, q >= first + pairs), 1, 0)

    def pair(q):
        return jnp.where(q < first, q, jnp.where(q < first + pairs, q - first, q - pairs))

    def fresh(q):
        return jnp.logical_or(q < first, jnp.logical_and(q >= 2 * first, q < first + pairs))

    def group(place):
        return lax.rem(mine + 1 + place, G)

    other_core = row + 1 - 2 * lax.rem(row, 2)
    same_core = [lax.rem(row + 2 * k, R) for k in range(1, R // 2)]

    def remote(src, dst, ssem, rsem, dev):
        return pltpu.make_async_remote_copy(
            src_ref=src, dst_ref=dst, send_sem=ssem, recv_sem=rsem,
            device_id=dev, device_id_type=MESH,
        )

    def both(*conds):
        return functools.reduce(jnp.logical_and, conds)

    def at_s(q):
        return lax.rem(q, DS)

    def at_r(q):
        return lax.rem(q, D)

    def send(make, q):
        @pl.when(q >= DS)
        def _():
            make(q - DS).wait_send()

        make(q).start()

    def live(q):
        return jnp.logical_and(q >= 0, q < Q)

    barrier = pltpu.get_barrier_semaphore()
    for k in range(1, R):
        pl.semaphore_signal(barrier, inc=1, device_id=(rpeer(k), col), device_id_type=MESH)
    for k in range(1, C):
        for r in (row, other_core):
            pl.semaphore_signal(barrier, inc=1, device_id=(r, cpeer(k)), device_id_type=MESH)
    cuts = sorted({0, min(1, pairs), min(2, pairs), pairs})
    early = min(2, first)

    def loads(i):
        cols = pl.ds(cuts[i] * 2 * W, (cuts[i + 1] - cuts[i]) * 2 * W)
        return (
            pltpu.make_async_copy(wd_hbm.at[cols], wd.at[cols], w_sem.at[0, i]),
            pltpu.make_async_copy(wg_hbm.at[:, cols], wg.at[:, cols], w_sem.at[1, i]),
            pltpu.make_async_copy(wu_hbm.at[:, cols], wu.at[:, cols], w_sem.at[2, i]),
        )

    for i in range(len(cuts) - 1):
        for load in loads(i):
            load.start()
    def keep(mask_ref, r, c):
        return jnp.full((BLK, BLK), mask_ref[r, c].astype(F32), F32).astype(BF16)

    def columns(p):
        return pl.ds(pl.multiple_of(p * (2 * W), 2 * W), 2 * W)

    def mask_pair(p):
        for i, cut in enumerate(cuts[:-1]):

            @pl.when(p == cut)
            def _():
                for load in loads(i):
                    load.wait()

        per = 2 * W // BLK
        for b in range(per):
            at = pl.ds(pl.multiple_of(p * (2 * W) + b * BLK, BLK), BLK)
            block = p * per + b
            for r in range(feats // BLK):
                f = slice(r * BLK, (r + 1) * BLK)
                wd[at, f] = wd[at, f] * keep(md_ref, r, block)
                wg[f, at] = wg[f, at] * keep(mg_ref, r, block)
                wu[f, at] = wu[f, at] * keep(mu_ref, r, block)

    og_all[row] = og_ref[...]
    x = x_ref[...].astype(F32)
    tok = lax.broadcasted_iota(jnp.int32, (rows, LANES), 0)
    lane = lax.broadcasted_iota(jnp.int32, (rows, LANES), 1)
    diag = tok == lane

    def to_lanes(column):
        return jnp.sum(jnp.where(diag, column, 0.0), axis=0, keepdims=True)

    def to_column(line):
        return jnp.sum(jnp.where(diag, line, 0.0), axis=1, keepdims=True)

    sq_mine[...] = to_lanes(jnp.sum(x * x, axis=1, keepdims=True))
    sq_all[0, col] = sq_mine[...]
    pl.semaphore_wait(barrier, R - 1 + 2 * (C - 1))

    def by_core(w):
        return (row, other_core)[w], range(1 - w, C)

    def sq_copy(w, src, dev):
        r, _ = by_core(w)
        return remote(sq_mine, sq_all.at[w, src], sq_s.at[w, dev], sq_r.at[w, src], (r, dev))

    x_copy_other = remote(x_ref, x_other, xo_s.at[0], xo_r.at[0], (other_core, col))
    for w in range(2):
        for k in by_core(w)[1]:
            sq_copy(w, col, cpeer(k)).start()
    x_copy_other.start()

    def tok_copy(kind, src, dev):
        blocks, ssem, _, rsem = kind
        return remote(blocks.at[src], blocks.at[src], ssem.at[dev], rsem.at[src], (dev, col))

    def tok_pass(kind, src):
        blocks, _, fsem, rsem = kind
        return remote(blocks.at[src], blocks.at[src], fsem.at[src], rsem.at[src], (other_core, col))

    og_kind = (og_all, og_s, og_f, og_r)
    nm_kind = (nm_all, nm_s, nm_f, nm_r)

    def tok_first(kind):
        for dev in same_core:
            tok_copy(kind, row, dev).start()

    def tok_second(kind, own):
        for src in same_core:

            @pl.when((src // RG == mine) == own)
            def _():
                tok_copy(kind, src, src).wait_recv()
                tok_pass(kind, src).start()

    def tok_last(kind, own):
        for k in range(1, R):
            src = rpeer(k)
            missing = jnp.logical_and(lax.rem(src, 2) != lax.rem(row, 2), (src // RG == mine) == own)
            if kind is nm_kind:
                missing = jnp.logical_and(missing, src != other_core)

            @pl.when(missing)
            def _():
                tok_copy(kind, src, src).wait_recv()

    tok_copy(og_kind, row, other_core).start()
    tok_first(og_kind)
    for p in range(early):
        mask_pair(jnp.int32(p))
    acc_d[...] = jnp.zeros_like(acc_d)
    acc_n[...] = jnp.zeros_like(acc_n)
    gain = gain_ref[...]

    def row_scale(w):
        for k in by_core(w)[1]:
            sq_copy(w, cpeer(k), cpeer(k)).wait_recv()
        total = sq_all[w, 0]
        for c in range(1, C):
            total = total + sq_all[w, c]
        return lax.rsqrt(to_column(total) / total_width + norm_eps)

    scale = row_scale(0)
    nm_all[row] = (x * scale * gain).astype(BF16)
    tok_first(nm_kind)
    x_copy_other.wait_recv()
    scale_other = row_scale(1)
    nm_all[other_core] = (x_other[...].astype(F32) * scale_other * gain).astype(BF16)

    def parts(q):
        p = pair(q)
        grp = group(place(q))
        cols = columns(p)

        @pl.when(jnp.logical_and(fresh(q), q >= early))
        def _():
            mask_pair(p)

        ogt = og_all[pl.ds(grp * RG, RG)].reshape(TG, feats)
        nmt = nm_all[pl.ds(grp * RG, RG)].reshape(TG, feats)
        for i in range(3):
            if i == 0:
                v = dot_nt(ogt, wd[cols, :])
            else:
                v = dot_nn(nmt, (wg, wu)[i - 1][:, cols])
            v = v.astype(BF16)
            for xx in range(NX):
                for h in range(2):
                    b = xx * 2 + h
                    xp[q, xx, h, i] = v[b * T : (b + 1) * T, :W]
            for h in range(2):
                zp[q, h, i] = v[h * NX * T : (h + 1) * NX * T, W:]

    def znb(step):
        return (row, (mz + step) * NX + mx)

    def along_x(k, out):
        dev = xpeer(k)
        return (mx, dev, k - 1) if out else (dev, dev, NX - k - 1)

    def x_copy(q, k, out):
        src, dev, i = along_x(k, out)
        return remote(
            xp.at[q, dev], xr.at[q, src], x_s.at[at_s(q), i], x_r.at[at_r(q), i],
            (row, mz * NX + dev),
        )

    def xc_copy(q, h, step):
        return remote(
            xp.at[q, mx, h], xc.at[q, h], xc_s.at[at_s(q), h], xc_r.at[at_r(q), h], znb(step)
        )

    def zc_copy(q, h, step):
        return remote(
            zp.at[q, h], zc.at[q, h], zc_s.at[at_s(q), h], zc_r.at[at_r(q), h], znb(step)
        )

    def zx_copy(q, k, out):
        src, dev, i = along_x(k, out)
        return remote(
            zp.at[q, half], zx.at[q, src], zx_s.at[at_s(q), i], zx_r.at[at_r(q), i],
            (row, mz * NX + dev),
        )

    def x_tokens(src, h):
        return pl.ds(pl.multiple_of((src * 2 + h) * T, T), T)

    def z_tokens(h):
        return pl.ds(pl.multiple_of(h * (NX * T), NX * T), NX * T)

    def axz_copy(q, h, step):
        block = agx.at[q, :, x_tokens(mx, h)]
        return remote(block, block, axz_s.at[at_s(q), h], axz_r.at[at_r(q), h], znb(step))

    def axx_copy(q, h, k, out):
        src, dev, i = along_x(k, out)
        block = agx.at[q, :, x_tokens(src, h)]
        return remote(
            block, block, axx_s.at[at_s(q), h, i], axx_r.at[at_r(q), h, i],
            (row, mz * NX + dev),
        )

    def az_copy(q, h, step):
        block = agz.at[q, :, z_tokens(h)]
        return remote(block, block, az_s.at[at_s(q), h], az_r.at[at_r(q), h], znb(step))

    def pointwise(gate, up, da):
        sig = jax.nn.sigmoid(gate)
        return (
            (gate * sig * up).astype(BF16),
            (da * up * sig * (1.0 + gate * (1.0 - sig))).astype(BF16),
            (da * gate * sig).astype(BF16),
        )

    def x_send(q):
        @pl.when(live(q))
        def _():
            for k in range(1, NX):
                send(lambda q: x_copy(q, k, True), q)

    def share_x(q, h):
        for k in range(1, NX):
            send(lambda q: axx_copy(q, h, k, True), q)

    def spread_x():
        for h, step, hops in ((0, 1, mz), (1, -1, NZ - 1 - mz)):
            q = s_now[0] - H * (NZ + hops)

            @pl.when(both(live(q), hops > 0))
            def _():
                axz_copy(q, h, -step).wait_recv()

                @pl.when(hops < NZ - 1)
                def _():
                    send(lambda q: axz_copy(q, h, step), q)

                share_x(q, h)

    def spread_z():
        for h, step, hops in ((0, 1, mz), (1, -1, NZ - 1 - mz)):
            q = s_now[0] - H * (NZ + hops)

            @pl.when(both(live(q), hops > 0))
            def _():
                az_copy(q, h, -step).wait_recv()

                @pl.when(hops < NZ - 1)
                def _():
                    send(lambda q: az_copy(q, h, step), q)

    def chain_x():
        for h, step, hops in ((1, 1, mz), (0, -1, NZ - 1 - mz)):
            q = s_now[0] - H * (1 + hops)

            @pl.when(both(live(q), hops > 0, hops < NZ - 1))
            def _():
                xc_copy(q, h, -step).wait_recv()
                xp[q, mx, h] = (xp[q, mx, h].astype(F32) + xc[q, h].astype(F32)).astype(BF16)
                send(lambda q: xc_copy(q, h, step), q)

    def chain_z():
        for h, step, hops in ((1, 1, mz), (0, -1, NZ - 1 - mz)):
            q = s_now[0] - H * hops

            @pl.when(both(live(q), hops > 0, hops < NZ - 1))
            def _():
                zc_copy(q, h, -step).wait_recv()
                zp[q, h] = (zp[q, h].astype(F32) + zc[q, h].astype(F32)).astype(BF16)
                send(lambda q: zc_copy(q, h, step), q)

    def sum_x(q):
        @pl.when(live(q))
        def _():
            for k in range(1, NX):
                x_copy(q, k, False).wait_recv()
            for h in range(2):
                v = xp[q, mx, h].astype(F32)
                for k in range(1, NX):
                    v = v + xr[q, xpeer(k), h].astype(F32)
                xp[q, mx, h] = v.astype(BF16)

            @pl.when(low)
            def _():
                send(lambda q: xc_copy(q, 1, 1), q)

            @pl.when(high)
            def _():
                send(lambda q: xc_copy(q, 0, -1), q)

    def finish_x(q):
        for h, at_end, step in ((0, low, 1), (1, high, -1)):

            @pl.when(both(live(q), at_end))
            def _():
                xc_copy(q, h, step).wait_recv()
                da, gate, up = (
                    xp[q, mx, h, i].astype(F32) + xc[q, h, i].astype(F32) for i in range(3)
                )
                for i, v in enumerate(pointwise(gate, up, da)):
                    agx[q, i, x_tokens(mx, h)] = v
                send(lambda q: axz_copy(q, h, step), q)
                share_x(q, h)

    def start_z(q):
        @pl.when(both(live(q), low))
        def _():
            send(lambda q: zc_copy(q, 1, 1), q)

        @pl.when(both(live(q), high))
        def _():
            send(lambda q: zc_copy(q, 0, -1), q)

    def exchange_z(q):
        for h, at_end, step in ((0, low, 1), (1, high, -1)):

            @pl.when(both(live(q), at_end))
            def _():
                zc_copy(q, h, step).wait_recv()
                zp[q, h] = (zp[q, h].astype(F32) + zc[q, h].astype(F32)).astype(BF16)
                for k in range(1, NX):
                    send(lambda q: zx_copy(q, k, True), q)

    def finish_z(q):
        for h, at_end, step in ((0, low, 1), (1, high, -1)):

            @pl.when(both(live(q), at_end))
            def _():
                for k in range(1, NX):
                    zx_copy(q, k, False).wait_recv()

                def summed(i):
                    v = zp[q, h, i].astype(F32)
                    for k in range(1, NX):
                        v = v + zx[q, xpeer(k), i].astype(F32)
                    return v

                da, gate, up = (summed(i) for i in range(3))
                for i, v in enumerate(pointwise(gate, up, da)):
                    agz[q, i, h * NX * T : (h + 1) * NX * T] = v
                send(lambda q: az_copy(q, h, step), q)

    def gather_x():
        for h, hops in ((0, mz), (1, NZ - 1 - mz)):
            q = s_now[0] - H * (NZ + 1 + hops)

            @pl.when(live(q))
            def _():
                for k in range(1, NX):
                    axx_copy(q, h, k, False).wait_recv()

    def out_copies(q):
        return (
            pltpu.make_async_copy(agx.at[q], agx_out.at[place(q), pair(q)], out_s.at[at_s(q), 0]),
            pltpu.make_async_copy(agz.at[q], agz_out.at[place(q), pair(q)], out_s.at[at_s(q), 1]),
        )

    def products(q):
        @pl.when(live(q))
        def _():
            @pl.when(q >= DS)
            def _():
                for copy in out_copies(q - DS):
                    copy.wait()

            for copy in out_copies(q):
                copy.start()
            grp = group(place(q))
            cols = columns(pair(q))

            def tokens(i):
                return jnp.concatenate([agx[q, i], agz[q, i]], axis=1)

            acc_d[grp] += dot_nn(tokens(0), wd[cols, :])
            acc_n[grp] += dot_nt(tokens(1), wg[:, cols]) + dot_nt(tokens(2), wu[:, cols])

    def drain(q):
        for k in range(1, NX):
            x_copy(q, k, True).wait_send()
            for h in range(2):
                axx_copy(q, h, k, True).wait_send()
        for h, step, hops in ((1, 1, mz), (0, -1, NZ - 1 - mz)):

            @pl.when(hops < NZ - 1)
            def _():
                xc_copy(q, h, step).wait_send()
                zc_copy(q, h, step).wait_send()
                axz_copy(q, 1 - h, step).wait_send()
                az_copy(q, 1 - h, step).wait_send()

        @pl.when(end)
        def _():
            for k in range(1, NX):
                zx_copy(q, k, True).wait_send()

        for copy in out_copies(q):
            copy.wait()

    def fin_copy(src, dev):
        return remote(
            fin_s.at[dev], fin_r.at[src], fin_ss.at[dev], fin_rs.at[src], (dev, col)
        )

    def fin_rows(r):
        return pl.ds(pl.multiple_of(lax.rem(r, RG) * rows, rows), rows)

    def fin_send(r):
        fin_s[r, 0] = acc_d[r // RG, fin_rows(r)].astype(BF16)
        fin_s[r, 1] = acc_n[r // RG, fin_rows(r)].astype(BF16)
        fin_copy(row, r).start()

    for kind in (og_kind, nm_kind):
        tok_second(kind, True)
    for kind in (og_kind, nm_kind):
        tok_last(kind, True)
    nm_outs = [
        pltpu.make_async_copy(
            blocks.at[pl.ds(group(g) * RG, RG)], dst.at[pl.ds(g * RG, RG)], tok_s.at[i, g]
        )
        for i, (blocks, dst) in enumerate(((nm_all, nm_out), (og_all, og_out)))
        for g in range(G)
    ]
    parts(0)
    s_now = [0]

    def one_step(s, carry):
        s_now[0] = s
        x_send(s)
        start_z(s)
        spread_x()
        gather_x()
        chain_x()
        sum_x(s - H)
        finish_x(s - H * NZ)

        @pl.when(s == min(2, first - 1))
        def _():
            for kind in (og_kind, nm_kind):
                tok_second(kind, False)

        @pl.when(s == first - 1)
        def _():
            for kind in (og_kind, nm_kind):
                tok_last(kind, False)
            for copy in nm_outs:
                copy.start()

        @pl.when(s + 1 < Q)
        def _():
            parts(s + 1)

        spread_z()
        chain_z()
        exchange_z(s - H * (NZ - 1))
        finish_z(s - H * NZ)
        products(s - H * (NZ + 1 + far))

        @pl.when(s == first + pairs - 1 + 2 * H * NZ)
        def _():
            for i in range(RG):
                fin_send(group(0) * RG + i)

        return carry

    lax.fori_loop(0, Q + 2 * H * NZ, one_step, 0)

    for k in range(1, RG):
        fin_send(mine * RG + lax.rem(row + k, RG))
    for copy in nm_outs:
        copy.wait()
    x_peer = x_other[...].astype(F32)
    part = acc_n[mine, fin_rows(other_core)]
    dt_other[...] = to_lanes(jnp.sum(part * gain * x_peer, axis=1, keepdims=True))

    def dt_copy(w, src, dev):
        r, _ = by_core(w)
        return remote(
            (dt_mine, dt_other)[w], dt_all.at[w, src], dt_s.at[w, dev], dt_r.at[w, src], (r, dev)
        )

    def gn_copy(src, dev):
        return remote(gn_mine, gn_all.at[src], gn_s.at[dev], gn_r.at[src], (dev, col))

    for k in by_core(1)[1]:
        dt_copy(1, col, cpeer(k)).start()
    down = acc_d[mine, fin_rows(row)]
    ngrad = acc_n[mine, fin_rows(row)]
    for k in range(1, R):
        src = rpeer(k)

        @pl.when(src != other_core)
        def _():
            fin_copy(src, src).wait_recv()

    def others(i):
        total = jnp.zeros((rows, feats), F32)
        for k in range(1, R // 2):
            for core in range(2):
                total = total + fin_r[lax.rem(row // 2 + k, R // 2) * 2 + core, i].astype(F32)
        return total

    down = down + others(0)
    ngrad = ngrad + others(1)
    x = x_ref[...].astype(F32)
    dt_mine[...] = to_lanes(jnp.sum(ngrad * gain * x, axis=1, keepdims=True))
    gn_mine[...] = jnp.sum(ngrad * x * scale + part * x_peer * scale_other, axis=0, keepdims=True)
    for k in by_core(0)[1]:
        dt_copy(0, col, cpeer(k)).start()
    for k in range(1, R):
        gn_copy(row, rpeer(k)).start()
    dt_all[0, col] = dt_mine[...]
    gn_all[row] = gn_mine[...]
    fin_copy(other_core, other_core).wait_recv()
    down = down + fin_r[other_core, 0].astype(F32)
    ngrad = ngrad + fin_r[other_core, 1].astype(F32)
    out_ref[...] = (x + down).astype(BF16)
    for dev in same_core:
        for kind in (og_kind, nm_kind):
            tok_copy(kind, row, dev).wait_send()
            tok_pass(kind, dev).wait_send()
    tok_copy(og_kind, row, other_core).wait_send()
    x_copy_other.wait_send()
    for k in range(1, R):
        fin_copy(row, rpeer(k)).wait_send()
    for w in range(2):
        for k in by_core(w)[1]:
            sq_copy(w, col, cpeer(k)).wait_send()
    for q in range(Q - DS, Q):
        drain(q)
    for w in range(2):
        for k in by_core(w)[1]:
            dt_copy(w, cpeer(k), cpeer(k)).wait_recv()
    dots = dt_all[0, 0] + dt_all[1, 0]
    for c in range(1, C):
        dots = dots + dt_all[0, c] + dt_all[1, c]
    dots = to_column(dots)
    ig_ref[...] = (
        og_ref[...].astype(F32)
        + scale * gain * ngrad
        - x * scale * scale * scale * dots / total_width
    ).astype(BF16)
    for k in range(1, R):
        gn_copy(rpeer(k), rpeer(k)).wait_recv()
    gain_sum = gn_all[0]
    for r in range(1, R):
        gain_sum = gain_sum + gn_all[r]
    gg_out[...] = gain_sum
    for k in range(1, R):
        gn_copy(row, rpeer(k)).wait_send()
    for w in range(2):
        for k in by_core(w)[1]:
            dt_copy(w, col, cpeer(k)).wait_send()


def wgrad_kernel(nm_ref, og_ref, agx_ref, agz_ref, mg_ref, mu_ref, md_ref,
                 lo_ref, ig_ref, gn_ref, gw_ref, uw_ref, dw_ref, lo_out, ig_out, gn_out):
    p = pl.program_id(0)

    @pl.when(p == 0)
    def _():
        lo_out[...] = lo_ref[...]
        ig_out[...] = ig_ref[...]
        gn_out[...] = gn_ref[...]

    step = agx_ref.shape[1]
    feats = nm_ref.shape[1]
    per = step * 2 * W // BLK

    def tokens(i):
        return jnp.concatenate(
            [
                jnp.concatenate([ref[g, k, i] for k in range(step) for ref in (agx_ref, agz_ref)], axis=1)
                for g in range(G)
            ],
            axis=0,
        )

    for i, mask, dst in ((1, mg_ref, gw_ref), (2, mu_ref, uw_ref)):
        w = dot_tn(nm_ref[...], tokens(i))
        for r in range(feats // BLK):
            for b in range(per):
                at = (slice(r * BLK, (r + 1) * BLK), slice(b * BLK, (b + 1) * BLK))
                dst[at] = (w[at] * mask[r, p * per + b].astype(F32)).astype(BF16)
    w = dot_tn(tokens(0), og_ref[...])
    for r in range(feats // BLK):
        for b in range(per):
            at = (slice(b * BLK, (b + 1) * BLK), slice(r * BLK, (r + 1) * BLK))
            dw_ref[at] = (w[at] * md_ref[r, p * per + b].astype(F32)).astype(BF16)


def shards(R, C, layer_input, norm_gain, w_gate, w_up, w_down,
           mask_gate, mask_up, mask_down, out_grad):
    rows, feats = layer_input.shape
    hidden = w_gate.shape[1]
    tokens = rows * R
    NX = 1
    while (2 * NX) * (2 * NX) <= C:
        NX *= 2
    NZ = C // NX
    pairs = hidden // (2 * W)
    Q = G * pairs
    D = ring(Q, NZ)
    TG = tokens // G
    T = TG // (2 * NX)
    mask_down = mask_down.T
    vm = pl.BlockSpec(memory_space=pltpu.VMEM)
    sm = pl.BlockSpec(memory_space=pltpu.SMEM)
    hbm = pl.BlockSpec(memory_space=pl.ANY)
    dma = pltpu.SemaphoreType.DMA
    V = pltpu.VMEM
    out_shapes = (
        ((rows, feats), BF16), ((rows, feats), BF16), ((1, feats), F32),
        ((G, pairs, 3, TG, W), BF16), ((G, pairs, 3, TG, W), BF16),
        ((R, rows, feats), BF16), ((R, rows, feats), BF16),
    )
    scratch = [
        V((feats, hidden), BF16), V((feats, hidden), BF16), V((hidden, feats), BF16),
        V((R, rows, feats), BF16), V((R, rows, feats), BF16),
        V((rows, feats), BF16), V((1, LANES), F32), V((2, C, 1, LANES), F32),
        V((Q, NX, 2, 3, T, W), BF16), V((Q, NX, 2, 3, T, W), BF16), V((Q, 2, 3, T, W), BF16),
        V((Q, 2, 3, NX * T, W), BF16), V((Q, 2, 3, NX * T, W), BF16),
        V((Q, NX, 3, NX * T, W), BF16),
        V((Q, 3, TG, W), BF16), V((Q, 3, TG, W), BF16),
        V((G, TG, feats), F32), V((G, TG, feats), F32),
        V((R, 2, rows, feats), BF16), V((R, 2, rows, feats), BF16),
        V((1, feats), F32), V((R, 1, feats), F32),
        V((1, LANES), F32), V((1, LANES), F32), V((2, C, 1, LANES), F32),
        dma((3, 3)),
        dma((R,)), dma((R,)), dma((R,)), dma((R,)), dma((R,)), dma((R,)),
        dma((1,)), dma((1,)), dma((2, C)), dma((2, C)),
        dma((DS, NX - 1)), dma((D, NX - 1)), dma((DS, 2)), dma((D, 2)), dma((DS, 2)), dma((D, 2)),
        dma((DS, NX - 1)), dma((D, NX - 1)), dma((DS, 2)), dma((D, 2)),
        dma((DS, 2, NX - 1)), dma((D, 2, NX - 1)), dma((DS, 2)), dma((D, 2)),
        dma((R,)), dma((R,)), dma((R,)), dma((R,)), dma((2, C)), dma((2, C)),
        dma((DS, 2)), dma((2, G)),
    ]
    layer_out, input_grad, gain_grad, agx, agz, nm, og = pl.pallas_call(
        functools.partial(layer_kernel, R, NZ, NX, float(feats * C)),
        out_shape=tuple(jax.ShapeDtypeStruct(s, t) for s, t in out_shapes),
        in_specs=[vm] * 3 + [sm] * 3 + [hbm] * 3,
        out_specs=tuple([vm] * 3 + [hbm] * 4),
        scratch_shapes=scratch,
        compiler_params=pltpu.CompilerParams(
            collective_id=0, has_side_effects=True, vmem_limit_bytes=67043328
        ),
    )(layer_input, norm_gain[None, :], out_grad, mask_gate, mask_up, mask_down,
      w_gate, w_up, w_down)

    whole = lambda p: (0, 0)
    step = 2 if pairs % 2 == 0 else 1
    gate_wgrad, up_wgrad, down_wgrad, layer_out, input_grad, gain_grad = pl.pallas_call(
        wgrad_kernel,
        grid=(pairs // step,),
        out_shape=(
            jax.ShapeDtypeStruct((feats, hidden), BF16),
            jax.ShapeDtypeStruct((feats, hidden), BF16),
            jax.ShapeDtypeStruct((hidden, feats), BF16),
            jax.ShapeDtypeStruct((rows, feats), BF16),
            jax.ShapeDtypeStruct((rows, feats), BF16),
            jax.ShapeDtypeStruct((1, feats), F32),
        ),
        in_specs=[
            pl.BlockSpec((tokens, feats), whole),
            pl.BlockSpec((tokens, feats), whole),
            pl.BlockSpec((G, step, 3, TG, W), lambda p: (0, p, 0, 0, 0)),
            pl.BlockSpec((G, step, 3, TG, W), lambda p: (0, p, 0, 0, 0)),
            sm, sm, sm,
            pl.BlockSpec((rows, feats), whole),
            pl.BlockSpec((rows, feats), whole),
            pl.BlockSpec((1, feats), whole),
        ],
        out_specs=(
            pl.BlockSpec((feats, step * 2 * W), lambda p: (0, p)),
            pl.BlockSpec((feats, step * 2 * W), lambda p: (0, p)),
            pl.BlockSpec((step * 2 * W, feats), lambda p: (p, 0)),
            pl.BlockSpec((rows, feats), whole),
            pl.BlockSpec((rows, feats), whole),
            pl.BlockSpec((1, feats), whole),
        ),
        compiler_params=pltpu.CompilerParams(vmem_limit_bytes=67043328),
    )(nm.reshape(tokens, feats), og.reshape(tokens, feats),
      agx, agz,
      mask_gate, mask_up, mask_down, layer_out, input_grad, gain_grad)
    return (layer_out, input_grad, gain_grad[0], gate_wgrad, up_wgrad, down_wgrad)


def solution(mesh):
    placed = (
        P("row", "col"),
        P("col"),
        P("col", "row"),
        P("col", "row"),
        P("row", "col"),
        P("col", "row"),
        P("col", "row"),
        P("row", "col"),
        P("row", "col"),
    )
    return jax.shard_map(
        functools.partial(shards, mesh.shape["row"], mesh.shape["col"]),
        mesh=mesh,
        in_specs=placed,
        out_specs=(
            P("row", "col"),
            P("row", "col"),
            P("col"),
            P("col", "row"),
            P("col", "row"),
            P("row", "col"),
        ),
        check_vma=False,
    )
```

```python
import functools

import jax
import jax.numpy as jnp
from jax import lax
from jax.experimental import pallas as pl
from jax.experimental.pallas import tpu as pltpu
from jax.sharding import PartitionSpec as P

BLK = 128
LANES = 128
MESH = pl.DeviceIdType.MESH
F32 = jnp.float32
BF16 = jnp.bfloat16
norm_eps = 1e-05


def dot_nn(left, right):
    return lax.dot_general(left, right, (((1,), (0,)), ((), ())), preferred_element_type=F32)


def dot_nt(left, right):
    return lax.dot_general(left, right, (((1,), (1,)), ((), ())), preferred_element_type=F32)


def dot_tn(left, right):
    return lax.dot_general(left, right, (((0,), (0,)), ((), ())), preferred_element_type=F32)


G = 2
W = 128
H = 2


DS = 2


def ring(Q, NZ):
    return min(Q, H * NZ)


def layer_kernel(
    R, NZ, NX, total_width,
    x_ref, gain_ref, og_ref, mg_ref, mu_ref, md_ref, wg_hbm, wu_hbm, wd_hbm,
    out_ref, ig_ref, gg_out, agx_out, agz_out, nm_out, og_out,
    wg, wu, wd, nm_all, og_all, x_other, sq_mine, sq_all,
    xp, xr, xc, zp, zc, zx, agx, agz,
    acc_d, acc_n, fin_s, fin_r, gn_mine, gn_all, dt_mine, dt_other, dt_all,
    w_sem, og_s, og_f, og_r, nm_s, nm_f, nm_r, xo_s, xo_r, sq_s, sq_r,
    x_s, x_r, xc_s, xc_r, zc_s, zc_r, zx_s, zx_r, axz_s, axz_r, axx_s, axx_r, az_s, az_r,
    fin_ss, fin_rs, gn_s, gn_r, dt_s, dt_r, out_s, tok_s,
):
    C = NZ * NX
    row = lax.axis_index("row")
    col = lax.axis_index("col")
    mz = col // NX
    mx = lax.rem(col, NX)
    rows, feats = x_ref.shape
    hidden = wg.shape[1]
    pairs = hidden // (2 * W)
    Q = G * pairs
    D = ring(Q, NZ)
    RG = R // G
    TG = RG * rows
    T = TG // (2 * NX)
    mine = row // RG
    low = mz == 0
    high = mz == NZ - 1
    end = jnp.logical_or(low, high)
    half = mz // (NZ - 1)
    far = jnp.maximum(mz, NZ - 1 - mz)

    def rpeer(k):
        return lax.rem(row + k, R)

    def cpeer(k):
        return lax.rem(col + k, C)

    def xpeer(k):
        return lax.rem(mx + k, NX)

    first = (pairs + 1) // 2

    def place(q):
        return jnp.where(jnp.logical_or(q < first, q >= first + pairs), 1, 0)

    def pair(q):
        return jnp.where(q < first, q, jnp.where(q < first + pairs, q - first, q - pairs))

    def fresh(q):
        return jnp.logical_or(q < first, jnp.logical_and(q >= 2 * first, q < first + pairs))

    def group(place):
        return lax.rem(mine + 1 + place, G)

    other_core = row + 1 - 2 * lax.rem(row, 2)
    same_core = [lax.rem(row + 2 * k, R) for k in range(1, R // 2)]

    def remote(src, dst, ssem, rsem, dev):
        return pltpu.make_async_remote_copy(
            src_ref=src, dst_ref=dst, send_sem=ssem, recv_sem=rsem,
            device_id=dev, device_id_type=MESH,
        )

    def both(*conds):
        return functools.reduce(jnp.logical_and, conds)

    def at_s(q):
        return lax.rem(q, DS)

    def at_r(q):
        return lax.rem(q, D)

    def send(make, q):
        @pl.when(q >= DS)
        def _():
            make(q - DS).wait_send()

        make(q).start()

    def live(q):
        return jnp.logical_and(q >= 0, q < Q)

    barrier = pltpu.get_barrier_semaphore()
    for k in range(1, R):
        pl.semaphore_signal(barrier, inc=1, device_id=(rpeer(k), col), device_id_type=MESH)
    for k in range(1, C):
        for r in (row, other_core):
            pl.semaphore_signal(barrier, inc=1, device_id=(r, cpeer(k)), device_id_type=MESH)
    cuts = sorted({0, min(1, pairs), min(2, pairs), pairs})
    early = min(2, first)

    def loads(i):
        cols = pl.ds(cuts[i] * 2 * W, (cuts[i + 1] - cuts[i]) * 2 * W)
        return (
            pltpu.make_async_copy(wd_hbm.at[cols], wd.at[cols], w_sem.at[0, i]),
            pltpu.make_async_copy(wg_hbm.at[:, cols], wg.at[:, cols], w_sem.at[1, i]),
            pltpu.make_async_copy(wu_hbm.at[:, cols], wu.at[:, cols], w_sem.at[2, i]),
        )

    for i in range(len(cuts) - 1):
        for load in loads(i):
            load.start()
    def keep(mask_ref, r, c):
        return jnp.full((BLK, BLK), mask_ref[r, c].astype(F32), F32).astype(BF16)

    def columns(p):
        return pl.ds(pl.multiple_of(p * (2 * W), 2 * W), 2 * W)

    def mask_pair(p):
        for i, cut in enumerate(cuts[:-1]):

            @pl.when(p == cut)
            def _():
                for load in loads(i):
                    load.wait()

        per = 2 * W // BLK
        for b in range(per):
            at = pl.ds(pl.multiple_of(p * (2 * W) + b * BLK, BLK), BLK)
            block = p * per + b
            for r in range(feats // BLK):
                f = slice(r * BLK, (r + 1) * BLK)
                wd[at, f] = wd[at, f] * keep(md_ref, r, block)
                wg[f, at] = wg[f, at] * keep(mg_ref, r, block)
                wu[f, at] = wu[f, at] * keep(mu_ref, r, block)

    og_all[row] = og_ref[...]
    x = x_ref[...].astype(F32)
    tok = lax.broadcasted_iota(jnp.int32, (rows, LANES), 0)
    lane = lax.broadcasted_iota(jnp.int32, (rows, LANES), 1)
    diag = tok == lane

    def to_lanes(column):
        return jnp.sum(jnp.where(diag, column, 0.0), axis=0, keepdims=True)

    def to_column(line):
        return jnp.sum(jnp.where(diag, line, 0.0), axis=1, keepdims=True)

    sq_mine[...] = to_lanes(jnp.sum(x * x, axis=1, keepdims=True))
    sq_all[0, col] = sq_mine[...]
    pl.semaphore_wait(barrier, R - 1 + 2 * (C - 1))

    def by_core(w):
        return (row, other_core)[w], range(1 - w, C)

    def sq_copy(w, src, dev):
        r, _ = by_core(w)
        return remote(sq_mine, sq_all.at[w, src], sq_s.at[w, dev], sq_r.at[w, src], (r, dev))

    x_copy_other = remote(x_ref, x_other, xo_s.at[0], xo_r.at[0], (other_core, col))
    for w in range(2):
        for k in by_core(w)[1]:
            sq_copy(w, col, cpeer(k)).start()
    x_copy_other.start()

    def tok_copy(kind, src, dev):
        blocks, ssem, _, rsem = kind
        return remote(blocks.at[src], blocks.at[src], ssem.at[dev], rsem.at[src], (dev, col))

    def tok_pass(kind, src):
        blocks, _, fsem, rsem = kind
        return remote(blocks.at[src], blocks.at[src], fsem.at[src], rsem.at[src], (other_core, col))

    og_kind = (og_all, og_s, og_f, og_r)
    nm_kind = (nm_all, nm_s, nm_f, nm_r)

    def tok_first(kind):
        for dev in same_core:
            tok_copy(kind, row, dev).start()

    def tok_second(kind, own):
        for src in same_core:

            @pl.when((src // RG == mine) == own)
            def _():
                tok_copy(kind, src, src).wait_recv()
                tok_pass(kind, src).start()

    def tok_last(kind, own):
        for k in range(1, R):
            src = rpeer(k)
            missing = jnp.logical_and(lax.rem(src, 2) != lax.rem(row, 2), (src // RG == mine) == own)
            if kind is nm_kind:
                missing = jnp.logical_and(missing, src != other_core)

            @pl.when(missing)
            def _():
                tok_copy(kind, src, src).wait_recv()

    tok_copy(og_kind, row, other_core).start()
    tok_first(og_kind)
    for p in range(early):
        mask_pair(jnp.int32(p))
    acc_d[...] = jnp.zeros_like(acc_d)
    acc_n[...] = jnp.zeros_like(acc_n)
    gain = gain_ref[...]

    def row_scale(w):
        for k in by_core(w)[1]:
            sq_copy(w, cpeer(k), cpeer(k)).wait_recv()
        total = sq_all[w, 0]
        for c in range(1, C):
            total = total + sq_all[w, c]
        return lax.rsqrt(to_column(total) / total_width + norm_eps)

    scale = row_scale(0)
    nm_all[row] = (x * scale * gain).astype(BF16)
    tok_first(nm_kind)
    x_copy_other.wait_recv()
    scale_other = row_scale(1)
    nm_all[other_core] = (x_other[...].astype(F32) * scale_other * gain).astype(BF16)

    def parts(q):
        p = pair(q)
        grp = group(place(q))
        cols = columns(p)

        @pl.when(jnp.logical_and(fresh(q), q >= early))
        def _():
            mask_pair(p)

        ogt = og_all[pl.ds(grp * RG, RG)].reshape(TG, feats)
        nmt = nm_all[pl.ds(grp * RG, RG)].reshape(TG, feats)
        for i in range(3):
            if i == 0:
                v = dot_nt(ogt, wd[cols, :])
            else:
                v = dot_nn(nmt, (wg, wu)[i - 1][:, cols])
            v = v.astype(BF16)
            for xx in range(NX):
                for h in range(2):
                    b = xx * 2 + h
                    xp[q, xx, h, i] = v[b * T : (b + 1) * T, :W]
            for h in range(2):
                zp[q, h, i] = v[h * NX * T : (h + 1) * NX * T, W:]

    def znb(step):
        return (row, (mz + step) * NX + mx)

    def along_x(k, out):
        dev = xpeer(k)
        return (mx, dev, k - 1) if out else (dev, dev, NX - k - 1)

    def x_copy(q, k, out):
        src, dev, i = along_x(k, out)
        return remote(
            xp.at[q, dev], xr.at[q, src], x_s.at[at_s(q), i], x_r.at[at_r(q), i],
            (row, mz * NX + dev),
        )

    def xc_copy(q, h, step):
        return remote(
            xp.at[q, mx, h], xc.at[q, h], xc_s.at[at_s(q), h], xc_r.at[at_r(q), h], znb(step)
        )

    def zc_copy(q, h, step):
        return remote(
            zp.at[q, h], zc.at[q, h], zc_s.at[at_s(q), h], zc_r.at[at_r(q), h], znb(step)
        )

    def zx_copy(q, k, out):
        src, dev, i = along_x(k, out)
        return remote(
            zp.at[q, half], zx.at[q, src], zx_s.at[at_s(q), i], zx_r.at[at_r(q), i],
            (row, mz * NX + dev),
        )

    def x_tokens(src, h):
        return pl.ds(pl.multiple_of((src * 2 + h) * T, T), T)

    def z_tokens(h):
        return pl.ds(pl.multiple_of(h * (NX * T), NX * T), NX * T)

    def axz_copy(q, h, step):
        block = agx.at[q, :, x_tokens(mx, h)]
        return remote(block, block, axz_s.at[at_s(q), h], axz_r.at[at_r(q), h], znb(step))

    def axx_copy(q, h, k, out):
        src, dev, i = along_x(k, out)
        block = agx.at[q, :, x_tokens(src, h)]
        return remote(
            block, block, axx_s.at[at_s(q), h, i], axx_r.at[at_r(q), h, i],
            (row, mz * NX + dev),
        )

    def az_copy(q, h, step):
        block = agz.at[q, :, z_tokens(h)]
        return remote(block, block, az_s.at[at_s(q), h], az_r.at[at_r(q), h], znb(step))

    def pointwise(gate, up, da):
        sig = jax.nn.sigmoid(gate)
        return (
            (gate * sig * up).astype(BF16),
            (da * up * sig * (1.0 + gate * (1.0 - sig))).astype(BF16),
            (da * gate * sig).astype(BF16),
        )

    def x_send(q):
        @pl.when(live(q))
        def _():
            for k in range(1, NX):
                send(lambda q: x_copy(q, k, True), q)

    def share_x(q, h):
        for k in range(1, NX):
            send(lambda q: axx_copy(q, h, k, True), q)

    def spread_x():
        for h, step, hops in ((0, 1, mz), (1, -1, NZ - 1 - mz)):
            q = s_now[0] - H * (NZ + hops)

            @pl.when(both(live(q), hops > 0))
            def _():
                axz_copy(q, h, -step).wait_recv()

                @pl.when(hops < NZ - 1)
                def _():
                    send(lambda q: axz_copy(q, h, step), q)

                share_x(q, h)

    def spread_z():
        for h, step, hops in ((0, 1, mz), (1, -1, NZ - 1 - mz)):
            q = s_now[0] - H * (NZ + hops)

            @pl.when(both(live(q), hops > 0))
            def _():
                az_copy(q, h, -step).wait_recv()

                @pl.when(hops < NZ - 1)
                def _():
                    send(lambda q: az_copy(q, h, step), q)

    def chain_x():
        for h, step, hops in ((1, 1, mz), (0, -1, NZ - 1 - mz)):
            q = s_now[0] - H * (1 + hops)

            @pl.when(both(live(q), hops > 0, hops < NZ - 1))
            def _():
                xc_copy(q, h, -step).wait_recv()
                xp[q, mx, h] = (xp[q, mx, h].astype(F32) + xc[q, h].astype(F32)).astype(BF16)
                send(lambda q: xc_copy(q, h, step), q)

    def chain_z():
        for h, step, hops in ((1, 1, mz), (0, -1, NZ - 1 - mz)):
            q = s_now[0] - H * hops

            @pl.when(both(live(q), hops > 0, hops < NZ - 1))
            def _():
                zc_copy(q, h, -step).wait_recv()
                zp[q, h] = (zp[q, h].astype(F32) + zc[q, h].astype(F32)).astype(BF16)
                send(lambda q: zc_copy(q, h, step), q)

    def sum_x(q):
        @pl.when(live(q))
        def _():
            for k in range(1, NX):
                x_copy(q, k, False).wait_recv()
            for h in range(2):
                v = xp[q, mx, h].astype(F32)
                for k in range(1, NX):
                    v = v + xr[q, xpeer(k), h].astype(F32)
                xp[q, mx, h] = v.astype(BF16)

                @pl.when((high, low)[h])
                def _():
                    send(lambda q: xc_copy(q, h, 2 * h - 1), q)

    def finish_x(q):
        for h, at_end, step in ((0, low, 1), (1, high, -1)):

            @pl.when(both(live(q), at_end))
            def _():
                xc_copy(q, h, step).wait_recv()
                da, gate, up = (
                    xp[q, mx, h, i].astype(F32) + xc[q, h, i].astype(F32) for i in range(3)
                )
                for i, v in enumerate(pointwise(gate, up, da)):
                    agx[q, i, x_tokens(mx, h)] = v
                send(lambda q: axz_copy(q, h, step), q)
                share_x(q, h)

    def start_z(q):
        @pl.when(both(live(q), low))
        def _():
            send(lambda q: zc_copy(q, 1, 1), q)

        @pl.when(both(live(q), high))
        def _():
            send(lambda q: zc_copy(q, 0, -1), q)

    def exchange_z(q):
        for h, at_end, step in ((0, low, 1), (1, high, -1)):

            @pl.when(both(live(q), at_end))
            def _():
                zc_copy(q, h, step).wait_recv()
                zp[q, h] = (zp[q, h].astype(F32) + zc[q, h].astype(F32)).astype(BF16)
                for k in range(1, NX):
                    send(lambda q: zx_copy(q, k, True), q)

    def finish_z(q):
        for h, at_end, step in ((0, low, 1), (1, high, -1)):

            @pl.when(both(live(q), at_end))
            def _():
                for k in range(1, NX):
                    zx_copy(q, k, False).wait_recv()

                def summed(i):
                    v = zp[q, h, i].astype(F32)
                    for k in range(1, NX):
                        v = v + zx[q, xpeer(k), i].astype(F32)
                    return v

                da, gate, up = (summed(i) for i in range(3))
                for i, v in enumerate(pointwise(gate, up, da)):
                    agz[q, i, h * NX * T : (h + 1) * NX * T] = v
                send(lambda q: az_copy(q, h, step), q)

    def gather_x():
        for h, hops in ((0, mz), (1, NZ - 1 - mz)):
            q = s_now[0] - H * (NZ + 1 + hops)

            @pl.when(live(q))
            def _():
                for k in range(1, NX):
                    axx_copy(q, h, k, False).wait_recv()

    def out_copies(q):
        return (
            pltpu.make_async_copy(agx.at[q], agx_out.at[place(q), pair(q)], out_s.at[at_s(q), 0]),
            pltpu.make_async_copy(agz.at[q], agz_out.at[place(q), pair(q)], out_s.at[at_s(q), 1]),
        )

    def products(q):
        @pl.when(live(q))
        def _():
            @pl.when(q >= DS)
            def _():
                for copy in out_copies(q - DS):
                    copy.wait()

            for copy in out_copies(q):
                copy.start()
            grp = group(place(q))
            cols = columns(pair(q))

            def tokens(i):
                return jnp.concatenate([agx[q, i], agz[q, i]], axis=1)

            acc_d[grp] += dot_nn(tokens(0), wd[cols, :])
            acc_n[grp] += dot_nt(tokens(1), wg[:, cols]) + dot_nt(tokens(2), wu[:, cols])

    def drain(q):
        for k in range(1, NX):
            x_copy(q, k, True).wait_send()
            for h in range(2):
                axx_copy(q, h, k, True).wait_send()
        for h, step, hops in ((1, 1, mz), (0, -1, NZ - 1 - mz)):

            @pl.when(hops < NZ - 1)
            def _():
                xc_copy(q, h, step).wait_send()
                zc_copy(q, h, step).wait_send()
                axz_copy(q, 1 - h, step).wait_send()
                az_copy(q, 1 - h, step).wait_send()

        @pl.when(end)
        def _():
            for k in range(1, NX):
                zx_copy(q, k, True).wait_send()

        for copy in out_copies(q):
            copy.wait()

    def fin_copy(src, dev):
        return remote(
            fin_s.at[dev], fin_r.at[src], fin_ss.at[dev], fin_rs.at[src], (dev, col)
        )

    def fin_rows(r):
        return pl.ds(pl.multiple_of(lax.rem(r, RG) * rows, rows), rows)

    def fin_send(r):
        fin_s[r, 0] = acc_d[r // RG, fin_rows(r)].astype(BF16)
        fin_s[r, 1] = acc_n[r // RG, fin_rows(r)].astype(BF16)
        fin_copy(row, r).start()

    for kind in (og_kind, nm_kind):
        tok_second(kind, True)
    for kind in (og_kind, nm_kind):
        tok_last(kind, True)
    nm_outs = [
        pltpu.make_async_copy(
            blocks.at[pl.ds(group(g) * RG, RG)], dst.at[pl.ds(g * RG, RG)], tok_s.at[i, g]
        )
        for i, (blocks, dst) in enumerate(((nm_all, nm_out), (og_all, og_out)))
        for g in range(G)
    ]
    parts(0)
    s_now = [0]

    def one_step(s, carry):
        s_now[0] = s
        x_send(s)
        start_z(s)
        spread_x()
        gather_x()
        chain_x()
        sum_x(s - H)
        finish_x(s - H * NZ)

        @pl.when(s == min(2, first - 1))
        def _():
            for kind in (og_kind, nm_kind):
                tok_second(kind, False)

        @pl.when(s == first - 1)
        def _():
            for kind in (og_kind, nm_kind):
                tok_last(kind, False)
            for copy in nm_outs:
                copy.start()

        @pl.when(s + 1 < Q)
        def _():
            parts(s + 1)

        spread_z()
        chain_z()
        exchange_z(s - H * (NZ - 1))
        finish_z(s - H * NZ)
        products(s - H * (NZ + 1 + far))

        @pl.when(s == first + pairs - 1 + 2 * H * NZ)
        def _():
            for i in range(RG):
                fin_send(group(0) * RG + i)

        return carry

    lax.fori_loop(0, Q + 2 * H * NZ, one_step, 0)

    for k in range(1, RG):
        fin_send(mine * RG + lax.rem(row + k, RG))
    for copy in nm_outs:
        copy.wait()
    x_peer = x_other[...].astype(F32)
    part = acc_n[mine, fin_rows(other_core)]
    dt_other[...] = to_lanes(jnp.sum(part * gain * x_peer, axis=1, keepdims=True))

    def dt_copy(w, src, dev):
        r, _ = by_core(w)
        return remote(
            (dt_mine, dt_other)[w], dt_all.at[w, src], dt_s.at[w, dev], dt_r.at[w, src], (r, dev)
        )

    def gn_copy(src, dev):
        return remote(gn_mine, gn_all.at[src], gn_s.at[dev], gn_r.at[src], (dev, col))

    for k in by_core(1)[1]:
        dt_copy(1, col, cpeer(k)).start()
    down = acc_d[mine, fin_rows(row)]
    ngrad = acc_n[mine, fin_rows(row)]
    for k in range(1, R):
        src = rpeer(k)

        @pl.when(src != other_core)
        def _():
            fin_copy(src, src).wait_recv()

    def others(i):
        total = jnp.zeros((rows, feats), F32)
        for k in range(1, R // 2):
            for core in range(2):
                total = total + fin_r[lax.rem(row // 2 + k, R // 2) * 2 + core, i].astype(F32)
        return total

    down = down + others(0)
    ngrad = ngrad + others(1)
    x = x_ref[...].astype(F32)
    dt_mine[...] = to_lanes(jnp.sum(ngrad * gain * x, axis=1, keepdims=True))
    gn_mine[...] = jnp.sum(ngrad * x * scale + part * x_peer * scale_other, axis=0, keepdims=True)
    for k in by_core(0)[1]:
        dt_copy(0, col, cpeer(k)).start()
    for k in range(1, R):
        gn_copy(row, rpeer(k)).start()
    dt_all[0, col] = dt_mine[...]
    gn_all[row] = gn_mine[...]
    fin_copy(other_core, other_core).wait_recv()
    down = down + fin_r[other_core, 0].astype(F32)
    ngrad = ngrad + fin_r[other_core, 1].astype(F32)
    out_ref[...] = (x + down).astype(BF16)
    for dev in same_core:
        for kind in (og_kind, nm_kind):
            tok_copy(kind, row, dev).wait_send()
            tok_pass(kind, dev).wait_send()
    tok_copy(og_kind, row, other_core).wait_send()
    x_copy_other.wait_send()
    for k in range(1, R):
        fin_copy(row, rpeer(k)).wait_send()
    for w in range(2):
        for k in by_core(w)[1]:
            sq_copy(w, col, cpeer(k)).wait_send()
    for q in range(Q - DS, Q):
        drain(q)
    for w in range(2):
        for k in by_core(w)[1]:
            dt_copy(w, cpeer(k), cpeer(k)).wait_recv()
    dots = dt_all[0, 0] + dt_all[1, 0]
    for c in range(1, C):
        dots = dots + dt_all[0, c] + dt_all[1, c]
    dots = to_column(dots)
    ig_ref[...] = (
        og_ref[...].astype(F32)
        + scale * gain * ngrad
        - x * scale * scale * scale * dots / total_width
    ).astype(BF16)
    for k in range(1, R):
        gn_copy(rpeer(k), rpeer(k)).wait_recv()
    gain_sum = gn_all[0]
    for r in range(1, R):
        gain_sum = gain_sum + gn_all[r]
    gg_out[...] = gain_sum
    for k in range(1, R):
        gn_copy(row, rpeer(k)).wait_send()
    for w in range(2):
        for k in by_core(w)[1]:
            dt_copy(w, col, cpeer(k)).wait_send()


def wgrad_kernel(nm_ref, og_ref, agx_ref, agz_ref, mg_ref, mu_ref, md_ref,
                 lo_ref, ig_ref, gn_ref, gw_ref, uw_ref, dw_ref, lo_out, ig_out, gn_out):
    p = pl.program_id(0)

    @pl.when(p == 0)
    def _():
        lo_out[...] = lo_ref[...]
        ig_out[...] = ig_ref[...]
        gn_out[...] = gn_ref[...]

    step = agx_ref.shape[1]
    feats = nm_ref.shape[1]
    per = step * 2 * W // BLK

    def tokens(i):
        return jnp.concatenate(
            [
                jnp.concatenate([ref[g, k, i] for k in range(step) for ref in (agx_ref, agz_ref)], axis=1)
                for g in range(G)
            ],
            axis=0,
        )

    for i, mask, dst in ((1, mg_ref, gw_ref), (2, mu_ref, uw_ref)):
        w = dot_tn(nm_ref[...], tokens(i))
        for r in range(feats // BLK):
            for b in range(per):
                at = (slice(r * BLK, (r + 1) * BLK), slice(b * BLK, (b + 1) * BLK))
                dst[at] = (w[at] * mask[r, p * per + b].astype(F32)).astype(BF16)
    w = dot_tn(tokens(0), og_ref[...])
    for r in range(feats // BLK):
        for b in range(per):
            at = (slice(b * BLK, (b + 1) * BLK), slice(r * BLK, (r + 1) * BLK))
            dw_ref[at] = (w[at] * md_ref[r, p * per + b].astype(F32)).astype(BF16)


def shards(R, C, layer_input, norm_gain, w_gate, w_up, w_down,
           mask_gate, mask_up, mask_down, out_grad):
    rows, feats = layer_input.shape
    hidden = w_gate.shape[1]
    tokens = rows * R
    NX = 1
    while (2 * NX) * (2 * NX) <= C:
        NX *= 2
    NZ = C // NX
    pairs = hidden // (2 * W)
    Q = G * pairs
    D = ring(Q, NZ)
    TG = tokens // G
    T = TG // (2 * NX)
    mask_down = mask_down.T
    vm = pl.BlockSpec(memory_space=pltpu.VMEM)
    sm = pl.BlockSpec(memory_space=pltpu.SMEM)
    hbm = pl.BlockSpec(memory_space=pl.ANY)
    dma = pltpu.SemaphoreType.DMA
    V = pltpu.VMEM
    out_shapes = (
        ((rows, feats), BF16), ((rows, feats), BF16), ((1, feats), F32),
        ((G, pairs, 3, TG, W), BF16), ((G, pairs, 3, TG, W), BF16),
        ((R, rows, feats), BF16), ((R, rows, feats), BF16),
    )
    scratch = [
        V((feats, hidden), BF16), V((feats, hidden), BF16), V((hidden, feats), BF16),
        V((R, rows, feats), BF16), V((R, rows, feats), BF16),
        V((rows, feats), BF16), V((1, LANES), F32), V((2, C, 1, LANES), F32),
        V((Q, NX, 2, 3, T, W), BF16), V((Q, NX, 2, 3, T, W), BF16), V((Q, 2, 3, T, W), BF16),
        V((Q, 2, 3, NX * T, W), BF16), V((Q, 2, 3, NX * T, W), BF16),
        V((Q, NX, 3, NX * T, W), BF16),
        V((Q, 3, TG, W), BF16), V((Q, 3, TG, W), BF16),
        V((G, TG, feats), F32), V((G, TG, feats), F32),
        V((R, 2, rows, feats), BF16), V((R, 2, rows, feats), BF16),
        V((1, feats), F32), V((R, 1, feats), F32),
        V((1, LANES), F32), V((1, LANES), F32), V((2, C, 1, LANES), F32),
        dma((3, 3)),
        dma((R,)), dma((R,)), dma((R,)), dma((R,)), dma((R,)), dma((R,)),
        dma((1,)), dma((1,)), dma((2, C)), dma((2, C)),
        dma((DS, NX - 1)), dma((D, NX - 1)), dma((DS, 2)), dma((D, 2)), dma((DS, 2)), dma((D, 2)),
        dma((DS, NX - 1)), dma((D, NX - 1)), dma((DS, 2)), dma((D, 2)),
        dma((DS, 2, NX - 1)), dma((D, 2, NX - 1)), dma((DS, 2)), dma((D, 2)),
        dma((R,)), dma((R,)), dma((R,)), dma((R,)), dma((2, C)), dma((2, C)),
        dma((DS, 2)), dma((2, G)),
    ]
    layer_out, input_grad, gain_grad, agx, agz, nm, og = pl.pallas_call(
        functools.partial(layer_kernel, R, NZ, NX, float(feats * C)),
        out_shape=tuple(jax.ShapeDtypeStruct(s, t) for s, t in out_shapes),
        in_specs=[vm] * 3 + [sm] * 3 + [hbm] * 3,
        out_specs=tuple([vm] * 3 + [hbm] * 4),
        scratch_shapes=scratch,
        compiler_params=pltpu.CompilerParams(
            collective_id=0, has_side_effects=True, vmem_limit_bytes=67043328
        ),
    )(layer_input, norm_gain[None, :], out_grad, mask_gate, mask_up, mask_down,
      w_gate, w_up, w_down)

    whole = lambda p: (0, 0)
    step = 2 if pairs % 2 == 0 else 1
    gate_wgrad, up_wgrad, down_wgrad, layer_out, input_grad, gain_grad = pl.pallas_call(
        wgrad_kernel,
        grid=(pairs // step,),
        out_shape=(
            jax.ShapeDtypeStruct((feats, hidden), BF16),
            jax.ShapeDtypeStruct((feats, hidden), BF16),
            jax.ShapeDtypeStruct((hidden, feats), BF16),
            jax.ShapeDtypeStruct((rows, feats), BF16),
            jax.ShapeDtypeStruct((rows, feats), BF16),
            jax.ShapeDtypeStruct((1, feats), F32),
        ),
        in_specs=[
            pl.BlockSpec((tokens, feats), whole),
            pl.BlockSpec((tokens, feats), whole),
            pl.BlockSpec((G, step, 3, TG, W), lambda p: (0, p, 0, 0, 0)),
            pl.BlockSpec((G, step, 3, TG, W), lambda p: (0, p, 0, 0, 0)),
            sm, sm, sm,
            pl.BlockSpec((rows, feats), whole),
            pl.BlockSpec((rows, feats), whole),
            pl.BlockSpec((1, feats), whole),
        ],
        out_specs=(
            pl.BlockSpec((feats, step * 2 * W), lambda p: (0, p)),
            pl.BlockSpec((feats, step * 2 * W), lambda p: (0, p)),
            pl.BlockSpec((step * 2 * W, feats), lambda p: (p, 0)),
            pl.BlockSpec((rows, feats), whole),
            pl.BlockSpec((rows, feats), whole),
            pl.BlockSpec((1, feats), whole),
        ),
        compiler_params=pltpu.CompilerParams(vmem_limit_bytes=67043328),
    )(nm.reshape(tokens, feats), og.reshape(tokens, feats),
      agx, agz,
      mask_gate, mask_up, mask_down, layer_out, input_grad, gain_grad)
    return (layer_out, input_grad, gain_grad[0], gate_wgrad, up_wgrad, down_wgrad)


def solution(mesh):
    placed = (
        P("row", "col"),
        P("col"),
        P("col", "row"),
        P("col", "row"),
        P("row", "col"),
        P("col", "row"),
        P("col", "row"),
        P("row", "col"),
        P("row", "col"),
    )
    return jax.shard_map(
        functools.partial(shards, mesh.shape["row"], mesh.shape["col"]),
        mesh=mesh,
        in_specs=placed,
        out_specs=(
            P("row", "col"),
            P("row", "col"),
            P("col"),
            P("col", "row"),
            P("col", "row"),
            P("row", "col"),
        ),
        check_vma=False,
    )
```
